256 devices in a mesh: member: 2 (over core), rep: 8 (over z), tensor: 16 (over x, y).
Axes of the slice: x: 4, y: 4, z: 8, core: 2. Of those that a mesh axis runs over, the one named last changes fastest.
Arguments:
- queries: bfloat16 [2, 64, 32, 128], P('member', 'rep'), parts along dimension 1, may hold values from -110 to 110
- keys: bfloat16 [2, 64, 8192, 128], P('member', 'rep', 'tensor'), parts along dimension 1, may hold values from -4.2 to 4.2
- values: bfloat16 [2, 64, 8192, 128], P('member', 'rep', 'tensor'), parts along dimension 1, may hold values from -6 to 6
- lengths: int32 [64], P('rep'), parts along dimension 0, may hold values from 256 to 2048, as said below
- targets: int32 [64], P('rep'), parts along dimension 0, may hold values from 0 to 16383
- residual: bfloat16 [2, 64, 4096], P('member', 'rep'), parts along dimension 1, may hold values from -32 to 32
- out_weight: bfloat16 [2, 4096, 4096], P('member', 'tensor'), may hold values from -0.75 to 0.75
- norm_gain: float32 [2, 4096], P('member'), may hold values from 0.5 to 1.5
- head_weight: bfloat16 [2, 4096, 16384], P('member', None, 'tensor'), may hold values from -0.2 to 0.2878906
Outputs:
- mean_logprobs: float32 [64, 16384], P(('rep', 'member'), 'tensor'), parts along dimension 0
- target_logprob: float32 [64], P(('rep', 'member')), parts along dimension 0
The draws below stay inside these ranges and needn't reach their ends.
There are 8 independent parts, one for each index of `rep`. The reference program is written for one: setup_inputs(seed, part) draws one part's arguments, and reference() takes and returns one part's arrays. A program takes and returns all parts, laid end to end along the dimension named above; an argument that names none is the same for every part. Nothing has to cross between parts.
Inputs may be any that keep to these rules, and one draw needn't show every extreme that they name: `lengths`: some row of every draw has all 2048 slots live.
All inputs are finite; a program needn't handle non-finite values.
Results may differ from the reference program's by a relative error of at most 0.004.
Values may be sent and summed in bfloat16 or wider, within the bound.
A program may use at most 64 MiB of HBM per device.

```python
import jax
import jax.numpy as jnp
from jax import lax

D = 4096
HEADS = 32
KV_HEADS = 4
HEAD_DIM = 128
CTX = 2048
ROWS = 8
VOCAB = 16384


def joint_draw(key):
    per_kv = HEADS // KV_HEADS
    key_query = jax.random.fold_in(key, 11)
    key_cache = jax.random.fold_in(key, 12)
    cache = jax.random.truncated_normal(key_cache, -4.0, 4.0, (2, ROWS, KV_HEADS, CTX, HEAD_DIM), jnp.float32)
    query_draw = jax.random.truncated_normal(key_query, -4.0, 4.0, (2, ROWS, KV_HEADS, per_kv, HEAD_DIM), jnp.float32)
    return (query_draw.reshape(2, ROWS, HEADS, HEAD_DIM), cache.reshape(2, ROWS, KV_HEADS * CTX, HEAD_DIM))


def draw_queries(key, part):
    return joint_draw(key)[0].astype(jnp.bfloat16)


def draw_keys(key, part):
    return joint_draw(key)[1].astype(jnp.bfloat16)


def draw_lengths(key, part):
    key_len = jax.random.fold_in(key, 21)
    key_row = jax.random.fold_in(key, 22)
    drawn = jax.random.randint(key_len, (ROWS,), CTX // 8, CTX + 1)
    full_row = jax.random.randint(key_row, (), 0, ROWS)
    return jnp.where(jnp.arange(ROWS, dtype=jnp.int32) == full_row, CTX, drawn).astype(jnp.int32)


def draw_residual(key, part):
    stream = 0.3 * jax.random.truncated_normal(jax.random.fold_in(key, 31), -4.0, 4.0, (2, ROWS, D), jnp.float32)
    return stream.astype(jnp.bfloat16)


def draw_head_weight(key, part):
    matrix = jax.random.truncated_normal(jax.random.fold_in(key, 41), -4.0, 4.0, (2, D, VOCAB), jnp.float32)
    matrix = matrix * (1.0 / 450.0 ** 0.5)
    return matrix.astype(jnp.bfloat16)


def touch_ends(values, own_key, low, largest):
    spot = [jax.random.randint(jax.random.fold_in(own_key, axis), (), 0, length) for axis, length in enumerate(values.shape)]
    main_axis = values.shape.index(max(values.shape))
    neighbour = spot[:main_axis] + [(spot[main_axis] + 1) % values.shape[main_axis]] + spot[main_axis + 1:]
    return values.at[tuple(spot)].set(low).at[tuple(neighbour)].set(largest)


def level_of(key, shape, shards, least, largest):
    def one(dim, parts):
        heights = jax.random.uniform(jax.random.fold_in(jax.random.fold_in(key, 6), dim), (parts,), jnp.float32, least / len(shards), largest / len(shards))
        return jnp.repeat(jnp.exp(heights), shape[dim] // parts).reshape((-1,) + (1,) * (len(shape) - dim - 1))

    factor_of = one(*shards[0])
    for cut in shards[1:]:
        factor_of = factor_of * one(*cut)
    return factor_of


def scatter_about(key, dims, spread, bound, cuts=(), kind=jnp.bfloat16):
    result = spread * jax.random.normal(key, dims, jnp.float32)
    if cuts:
        result = result * level_of(key, dims, cuts, -0.22, 0.18)
    return jnp.clip(result, -bound, bound).astype(kind)


def setup_inputs(seed: int = 0, part: int = 0) -> dict:
    streams_of = jax.random.split(jax.random.key(seed), 10)
    part_keys = jax.random.split(jax.random.fold_in(streams_of[9], part), 10)
    queries = draw_queries(jax.random.fold_in(jax.random.fold_in(streams_of[9], part), 71), part)
    keys = draw_keys(jax.random.fold_in(jax.random.fold_in(streams_of[9], part), 71), part)
    values = scatter_about(part_keys[2], (2, ROWS, KV_HEADS * CTX, HEAD_DIM), 1.0, 6.0, ((0, 2), (2, 16)))
    lengths = draw_lengths(jax.random.fold_in(jax.random.fold_in(streams_of[9], part), 71), part)
    targets = touch_ends(jax.random.randint(part_keys[4], (ROWS,), 0, VOCAB), jax.random.fold_in(part_keys[4], 1), 0, VOCAB - 1).astype(jnp.int32)
    residual = draw_residual(jax.random.fold_in(jax.random.fold_in(streams_of[9], part), 71), part)
    out_weight = scatter_about(streams_of[6], (2, HEADS * HEAD_DIM, D), 64 ** -0.5, 0.75, ((0, 2), (1, 16)))
    norm_gain = jnp.clip(1.0 + 0.1 * jax.random.normal(streams_of[7], (2, D), jnp.float32), 0.5, 1.5)
    head_weight = draw_head_weight(jax.random.fold_in(streams_of[9], 71), part)
    return dict(queries=queries, keys=keys, values=values, lengths=lengths, targets=targets, residual=residual, out_weight=out_weight, norm_gain=norm_gain, head_weight=head_weight)


def reference(queries, keys, values, lengths, targets, residual, out_weight, norm_gain, head_weight):
    per_kv = HEADS // KV_HEADS
    slot_pos = jnp.arange(CTX, dtype=jnp.int32)
    live = (slot_pos[None, :] < lengths[:, None])[:, None, None, :]
    scale_factor = 1.0 / HEAD_DIM ** 0.5
    results = []
    for member in range(2):
        query_all = queries[member].astype(jnp.float32).reshape(ROWS, KV_HEADS, per_kv, HEAD_DIM)
        key_all = keys[member].astype(jnp.float32).reshape(ROWS, KV_HEADS, CTX, HEAD_DIM)
        value_all = values[member].astype(jnp.float32).reshape(ROWS, KV_HEADS, CTX, HEAD_DIM)
        scores = jnp.einsum('rgqd,rgcd->rgqc', query_all, key_all) * scale_factor
        scores = jnp.where(live, scores, jnp.float32(-1e+30))
        top_score = lax.optimization_barrier(jnp.max(scores, axis=-1))
        weights = jnp.where(live, jnp.exp(scores - top_score[..., None]), jnp.float32(0.0))
        weight_total = lax.optimization_barrier(jnp.sum(weights, axis=-1))
        rounded = lax.optimization_barrier(weights.astype(jnp.bfloat16)).astype(jnp.float32)
        weighted = jnp.einsum('rgqc,rgcd->rgqd', rounded, value_all)
        attended = (weighted / weight_total[..., None]).reshape(ROWS, HEADS * HEAD_DIM).astype(jnp.bfloat16)
        projected = jnp.dot(attended, out_weight[member], preferred_element_type=jnp.float32)
        hidden = residual[member].astype(jnp.float32) + projected
        normed = hidden * lax.rsqrt(lax.optimization_barrier(jnp.mean(hidden * hidden, axis=-1, keepdims=True)) + 1e-05) * norm_gain[member]
        normed = normed.astype(jnp.bfloat16)
        logits = jnp.dot(normed, head_weight[member], preferred_element_type=jnp.float32)
        top_logit = lax.optimization_barrier(jnp.max(logits, axis=-1, keepdims=True))
        log_total = top_logit + jnp.log(lax.optimization_barrier(jnp.sum(jnp.exp(logits - top_logit), axis=-1, keepdims=True)))
        results.append(logits - log_total)
    mean_logprobs = 0.5 * (results[0] + results[1])
    target_logprob = jnp.take_along_axis(mean_logprobs, targets[:, None].astype(jnp.int32), axis=1)[:, 0]
    return (mean_logprobs, target_logprob)
```

```python
import functools

import jax
import jax.numpy as jnp
from jax import lax
from jax.experimental import pallas as pl
from jax.experimental.pallas import tpu as pltpu
from jax.sharding import PartitionSpec as P

HEADS = 32
KV_HEADS = 4
SIDE = 4
HBM = pltpu.MemorySpace.HBM

OFFSETS = sorted(
    [(dx, dy) for dx in range(SIDE) for dy in range(SIDE) if (dx, dy) != (0, 0)],
    key=lambda o: -(min(o[0], SIDE - o[0]) + min(o[1], SIDE - o[1])),
)


def slot_of(dx, dy):
    return (dx % SIDE) * SIDE + dy % SIDE


def step_kernel(
    q_hbm, k_hbm, v_hbm, len_hbm, tgt_hbm, res_hbm, wo_hbm, gain_hbm, wh_hbm,
    out_ref, tout_ref,
    q_ref, k_ref, v_ref, len_ref, tgt_ref, res_ref, wo_ref, gain_ref, inv_ref, wh_ref,
    att_send, att_recv, rs_send, rs_recv, hg_ref, lg_ref, lg_recv, stat_ref,
    in_sem, k_sem, v_sem, wh_sem,
    att_ssem, att_rsem, rs_ssem, rs_rsem, ag_ssem, ag_rsem, lg_ssem, lg_rsem, st_ssem, st_rsem,
):
    me = lax.axis_index("tensor")
    member = lax.axis_index("member")
    col, row = me // SIDE, me % SIDE
    rows, span, depth = k_ref.shape
    heads = HEADS // KV_HEADS
    width = wo_ref.shape[0]
    f32, bf16 = jnp.float32, jnp.bfloat16

    def peer(dx, dy):
        return (col + dx) % SIDE * SIDE + (row + dy) % SIDE

    small = [
        pltpu.make_async_copy(q_hbm.at[0, :, pl.ds(col * heads, heads), :], q_ref, in_sem.at[0]),
        pltpu.make_async_copy(len_hbm, len_ref, in_sem.at[1]),
        pltpu.make_async_copy(tgt_hbm, tgt_ref, in_sem.at[2]),
        pltpu.make_async_copy(
            res_hbm.at[0, :, pl.ds(pl.multiple_of(me * width, width), width)], res_ref, in_sem.at[3]
        ),
        pltpu.make_async_copy(gain_hbm, gain_ref, in_sem.at[4]),
        pltpu.make_async_copy(wo_hbm.at[0], wo_ref, in_sem.at[5]),
    ]
    k_copy = [
        pltpu.make_async_copy(k_hbm.at[0, r], k_ref.at[r], k_sem.at[r]) for r in range(rows)
    ]
    v_copy = [
        pltpu.make_async_copy(v_hbm.at[0, r], v_ref.at[r], v_sem.at[r]) for r in range(rows)
    ]
    chunks = wh_ref.shape[0] // width
    w_copy = [
        pltpu.make_async_copy(
            wh_hbm.at[0, pl.ds(c * width, width), :], wh_ref.at[pl.ds(c * width, width), :], wh_sem.at[c]
        )
        for c in range(chunks)
    ]
    small[0].start()
    small[1].start()
    for c in k_copy + v_copy:
        c.start()
    for c in small[2:]:
        c.start()

    barrier = pltpu.get_barrier_semaphore()
    for dx, dy in OFFSETS + [(0, 0)]:
        for other in range(2):
            if (dx, dy, other) == (0, 0, 0):
                continue
            pl.semaphore_signal(
                barrier,
                inc=1,
                device_id={"member": (member + other) % 2, "tensor": peer(dx, dy)},
                device_id_type=pl.DeviceIdType.MESH,
            )
    for c in w_copy:
        c.start()

    small[0].wait()
    small[1].wait()
    slot = row * span + lax.broadcasted_iota(jnp.int32, (heads, span), 1)
    lane = lax.broadcasted_iota(jnp.int32, (heads, depth), 1)
    scores, lives = [], []
    for r in range(rows):
        k_copy[r].wait()
        s = lax.dot_general(
            q_ref[r], k_ref[r], (((1,), (1,)), ((), ())), preferred_element_type=f32
        ) * (1.0 / depth**0.5)
        live = slot < len_ref[r]
        scores.append(jnp.where(live, s, f32(-1e30)))
        lives.append(live)
    for r in range(rows):
        top = jnp.max(scores[r], axis=-1, keepdims=True)
        w = jnp.where(lives[r], jnp.exp(scores[r] - top), f32(0.0))
        total = jnp.sum(w, axis=-1, keepdims=True)
        v_copy[r].wait()
        o = jnp.dot(w.astype(bf16), v_ref[r], preferred_element_type=f32)
        att_send[pl.ds(r, heads, stride=2 * rows), :] = o
        att_send[pl.ds(rows + r, heads, stride=2 * rows), :] = jnp.where(
            lane < depth // 2, top, total
        )

    pl.semaphore_wait(barrier, 31)
    block = 4 * rows
    att_copy = []
    for dy in (2, 1, 3):
        to = (row + dy) % SIDE
        att_copy.append(
            pltpu.make_async_remote_copy(
                src_ref=att_send.at[pl.ds(pl.multiple_of(to * block, block), block), :],
                dst_ref=att_recv.at[SIDE - dy - 1],
                send_sem=att_ssem.at[dy - 1],
                recv_sem=att_rsem.at[SIDE - dy - 1],
                device_id={"tensor": col * SIDE + to},
                device_id_type=pl.DeviceIdType.MESH,
            )
        )
        att_copy[-1].start()
    small[4].wait()
    inv_ref[...] = 1.0 / (gain_ref[...] * gain_ref[...])
    small[5].wait()
    small[2].wait()
    small[3].wait()
    parts = [att_send[pl.ds(pl.multiple_of(row * block, block), block), :]]
    for c in att_copy:
        c.wait_recv()
    for i in range(SIDE - 1):
        parts.append(att_recv[i])
    attended = []
    for h in range(2):
        base = 2 * h * rows
        stats = [p[base + rows : base + 2 * rows] for p in parts]
        peak = functools.reduce(jnp.maximum, stats)
        num, den = 0.0, 0.0
        for p, st in zip(parts, stats):
            scale = jnp.exp(st - peak)[:, 0:1]
            num = num + scale * p[base : base + rows]
            den = den + scale * st[:, depth // 2 : depth // 2 + 1]
        attended.append(num / den)
    attended = jnp.concatenate(attended, axis=1).astype(bf16)

    def project(t):
        return jnp.dot(
            attended,
            wo_ref[:, pl.ds(pl.multiple_of(t * width, width), width)],
            preferred_element_type=f32,
        )

    rs_copy = []
    for dx, dy in OFFSETS:
        t = peer(dx, dy)
        here, there = slot_of(dx, dy) - 1, slot_of(-dx, -dy) - 1
        rs_send[here] = project(t).astype(bf16)
        rs_copy.append(
            pltpu.make_async_remote_copy(
                src_ref=rs_send.at[here],
                dst_ref=rs_recv.at[there],
                send_sem=rs_ssem.at[here],
                recv_sem=rs_rsem.at[there],
                device_id={"tensor": t},
                device_id_type=pl.DeviceIdType.MESH,
            )
        )
        rs_copy[-1].start()
    hidden = project(me) + res_ref[...].astype(f32)
    for c in rs_copy[::-1]:
        c.wait_recv()
    for i in range(rs_recv.shape[0]):
        hidden = hidden + rs_recv[i].astype(f32)
    gain = gain_ref[:, pl.ds(pl.multiple_of(me * width, width), width)]
    hg_ref[0] = (hidden * gain).astype(bf16)
    ag_copy = {}
    for dx, dy in OFFSETS:
        here, there = slot_of(dx, dy), slot_of(-dx, -dy)
        ag_copy[there] = pltpu.make_async_remote_copy(
            src_ref=hg_ref.at[0],
            dst_ref=hg_ref.at[there],
            send_sem=ag_ssem.at[there - 1],
            recv_sem=ag_rsem.at[there - 1],
            device_id={"tensor": peer(dx, dy)},
            device_id_type=pl.DeviceIdType.MESH,
        )
        ag_copy[there].start()

    for c in w_copy:
        c.wait()
    logits, square = 0.0, 0.0
    for dx, dy in [(0, 0)] + OFFSETS[::-1]:
        t, k = peer(dx, dy), slot_of(dx, dy)
        if k:
            ag_copy[k].wait_recv()
        here = pl.multiple_of(t * width, width)
        part = hg_ref[k]
        logits = logits + jnp.dot(part, wh_ref[pl.ds(here, width), :], preferred_element_type=f32)
        wide = part.astype(f32)
        square = square + wide * wide * inv_ref[:, pl.ds(here, width)]
    mean_square = jnp.sum(square, axis=-1, keepdims=True) * (1.0 / (chunks * width))
    logits = logits * lax.rsqrt(mean_square + 1e-05)
    half = rows // 2
    lg_ref[0] = logits[:half]
    lg_ref[1] = logits[half:]
    lg_copy = pltpu.make_async_remote_copy(
        src_ref=lg_ref.at[1 - member],
        dst_ref=lg_recv,
        send_sem=lg_ssem,
        recv_sem=lg_rsem,
        device_id={"member": 1 - member},
        device_id_type=pl.DeviceIdType.MESH,
    )
    lg_copy.start()

    vocab = logits.shape[1]
    ids = me * vocab + lax.broadcasted_iota(jnp.int32, (rows, vocab), 1)
    sub = lax.broadcasted_iota(jnp.int32, (rows, 1), 0)
    want = jnp.zeros((rows, 1), jnp.int32)
    for r in range(rows):
        want = jnp.where(sub == r, tgt_ref[r], want)
    pick = jnp.sum(jnp.where(ids == want, logits, f32(0.0)), axis=-1, keepdims=True)
    top = jnp.max(logits, axis=-1, keepdims=True)
    lse = top + jnp.log(jnp.sum(jnp.exp(logits - top), axis=-1, keepdims=True))
    lanes = lax.broadcasted_iota(jnp.int32, (rows, 128), 1)
    subs = lax.broadcasted_iota(jnp.int32, (rows, 128), 0)
    spread = jnp.where(lanes < 64, lse, pick)
    stat_ref[0] = jnp.sum(
        jnp.where(lanes // 8 % 8 == subs, spread, f32(0.0)), axis=0, keepdims=True
    )
    st_copy = []
    for dx, dy in OFFSETS + [(0, 0)]:
        for other in range(2):
            there = slot_of(-dx, -dy) + SIDE * SIDE * other
            if there == 0:
                continue
            st_copy.append(
                pltpu.make_async_remote_copy(
                    src_ref=stat_ref.at[0],
                    dst_ref=stat_ref.at[there],
                    send_sem=st_ssem.at[there - 1],
                    recv_sem=st_rsem.at[there - 1],
                    device_id={"member": (member + other) % 2, "tensor": peer(dx, dy)},
                    device_id_type=pl.DeviceIdType.MESH,
                )
            )
            st_copy[-1].start()
    lg_copy.wait_recv()
    mean_logits = 0.5 * (lg_ref[member] + lg_recv[...])
    for c in st_copy[::-1]:
        c.wait_recv()
    log_total, target = 0.0, 0.0
    for other in range(2):
        got = [stat_ref[other * SIDE * SIDE + i] for i in range(SIDE * SIDE)]
        peak = functools.reduce(jnp.maximum, got)
        log_total = log_total + 0.5 * (peak + jnp.log(sum(jnp.exp(g - peak) for g in got)))
        target = target + 0.5 * sum(got)
    lanes = lax.broadcasted_iota(jnp.int32, (half, 128), 1)
    mine = 8 * (member * half + lax.broadcasted_iota(jnp.int32, (half, 128), 0))
    shift = jnp.sum(jnp.where(lanes == mine, log_total, f32(0.0)), axis=-1, keepdims=True)
    chosen = jnp.sum(jnp.where(lanes == mine + 64, target, f32(0.0)), axis=-1, keepdims=True)
    out_ref[...] = mean_logits - shift
    tout_ref[...] = jnp.broadcast_to(chosen - shift, (half, 128))

    for c in att_copy + rs_copy + list(ag_copy.values()) + [lg_copy] + st_copy:
        c.wait_send()


def local(queries, keys, values, lengths, targets, residual, out_weight, norm_gain, head_weight):
    rows, span, depth = keys.shape[1:]
    width, model = out_weight.shape[1:]
    vocab = head_weight.shape[2]
    peers = SIDE * SIDE - 1
    heads = HEADS // KV_HEADS
    f32, bf16 = jnp.float32, jnp.bfloat16
    dma = pltpu.SemaphoreType.DMA
    out, target = pl.pallas_call(
        step_kernel,
        out_shape=(
            jax.ShapeDtypeStruct((rows // 2, vocab), f32),
            jax.ShapeDtypeStruct((rows // 2, 128), f32),
        ),
        in_specs=[pl.BlockSpec(memory_space=HBM)] * 9,
        out_specs=(
            pl.BlockSpec(memory_space=pltpu.MemorySpace.VMEM),
            pl.BlockSpec(memory_space=pltpu.MemorySpace.VMEM),
        ),
        scratch_shapes=[
            pltpu.VMEM((rows, heads, depth), bf16),
            pltpu.VMEM((rows, span, depth), bf16),
            pltpu.VMEM((rows, span, depth), bf16),
            pltpu.SMEM((rows,), jnp.int32),
            pltpu.SMEM((rows,), jnp.int32),
            pltpu.VMEM((rows, width), bf16),
            pltpu.VMEM((width, model), bf16),
            pltpu.VMEM((1, model), f32),
            pltpu.VMEM((1, model), f32),
            pltpu.VMEM((model, vocab), bf16),
            pltpu.VMEM((2 * heads * rows, depth), f32),
            pltpu.VMEM((SIDE - 1, 4 * rows, depth), f32),
            pltpu.VMEM((peers, rows, width), bf16),
            pltpu.VMEM((peers, rows, width), bf16),
            pltpu.VMEM((peers + 1, rows, width), bf16),
            pltpu.VMEM((2, rows // 2, vocab), f32),
            pltpu.VMEM((rows // 2, vocab), f32),
            pltpu.VMEM((2 * (peers + 1), 1, 128), f32),
            dma((6,)), dma((rows,)), dma((rows,)), dma((peers + 1,)),
            dma((SIDE - 1,)), dma((SIDE - 1,)),
            dma((peers,)), dma((peers,)),
            dma((peers,)), dma((peers,)),
            dma, dma,
            dma((2 * peers + 1,)), dma((2 * peers + 1,)),
        ],
        compiler_params=pltpu.CompilerParams(
            collective_id=0, has_side_effects=True, vmem_limit_bytes=62 << 20
        ),
        name="decode_step",
    )(queries, keys, values, lengths, targets, residual, out_weight, norm_gain, head_weight)
    return out, target[:, 0]


def solution(mesh):
    placed = (
        P("member", "rep", None, None),
        P("member", "rep", "tensor", None),
        P("member", "rep", "tensor", None),
        P("rep"),
        P("rep"),
        P("member", "rep", None),
        P("member", "tensor", None),
        P("member", None),
        P("member", None, "tensor"),
    )
    return jax.shard_map(
        local,
        mesh=mesh,
        in_specs=placed,
        out_specs=(P(("rep", "member"), "tensor"), P(("rep", "member"))),
        check_vma=False,
    )
```

```python
import functools

import jax
import jax.numpy as jnp
from jax import lax
from jax.experimental import pallas as pl
from jax.experimental.pallas import tpu as pltpu
from jax.sharding import PartitionSpec as P

HEADS = 32
KV_HEADS = 4
SIDE = 4
CHUNKS = 4
HBM = pltpu.MemorySpace.HBM


def hops(dx, dy):
    return min(dx, SIDE - dx) + min(dy, SIDE - dy)


OFFSETS = sorted(
    [(dx, dy) for dx in range(SIDE) for dy in range(SIDE) if (dx, dy) != (0, 0)],
    key=lambda o: -hops(*o),
)


def slot_of(dx, dy):
    return (dx % SIDE) * SIDE + dy % SIDE


def step_kernel(
    q_hbm, k_hbm, v_hbm, len_hbm, tgt_hbm, res_hbm, wo_hbm, gain_hbm, wh_hbm,
    out_ref, tout_ref,
    q_ref, k_ref, v_ref, len_ref, tgt_ref, res_ref, wo_ref, gain_ref, inv_ref, wh_ref,
    res_other, gain_other, att_send, att_recv, rs_send, rs_recv, ag_ref, hg_ref, lg_ref, lg_recv, stat_ref,
    in_sem, k_sem, v_sem, wh_sem,
    side_ssem, side_rsem, att_ssem, att_rsem, rs_ssem, rs_rsem, ag_ssem, ag_rsem, lg_ssem, lg_rsem, st_ssem, st_rsem,
):
    me = lax.axis_index("tensor")
    member = lax.axis_index("member")
    col, row = me // SIDE, me % SIDE
    rows, span, depth = k_ref.shape
    heads = HEADS // KV_HEADS
    width = wo_ref.shape[0]
    f32, bf16 = jnp.float32, jnp.bfloat16

    def peer(dx, dy):
        return (col + dx) % SIDE * SIDE + (row + dy) % SIDE

    small = [
        pltpu.make_async_copy(q_hbm.at[0, :, pl.ds(col * heads, heads), :], q_ref, in_sem.at[0]),
        pltpu.make_async_copy(len_hbm, len_ref, in_sem.at[1]),
        pltpu.make_async_copy(tgt_hbm, tgt_ref, in_sem.at[2]),
        pltpu.make_async_copy(
            res_hbm.at[0, :, pl.ds(pl.multiple_of(me * width, width), width)], res_ref, in_sem.at[3]
        ),
        pltpu.make_async_copy(gain_hbm, gain_ref, in_sem.at[4]),
        pltpu.make_async_copy(wo_hbm.at[0], wo_ref, in_sem.at[5]),
    ]
    half = rows // 2
    k_copy, v_copy = [
        [
            pltpu.make_async_copy(
                hbm.at[0, pl.ds(i * half, half)], ref.at[pl.ds(i * half, half)], sem.at[i]
            )
            for i in range(2)
        ]
        for hbm, ref, sem in ((k_hbm, k_ref, k_sem), (v_hbm, v_ref, v_sem))
    ]
    model = wh_ref.shape[0]
    chunk = model // CHUNKS
    w_copy = [
        pltpu.make_async_copy(
            wh_hbm.at[0, pl.ds(c * chunk, chunk), :], wh_ref.at[pl.ds(c * chunk, chunk), :], wh_sem.at[c]
        )
        for c in range(CHUNKS)
    ]
    small[0].start()
    small[1].start()
    for c in k_copy + v_copy:
        c.start()
    for c in small[2:]:
        c.start()

    barrier = pltpu.get_barrier_semaphore()
    for dx, dy in OFFSETS + [(0, 0)]:
        for other in range(2):
            if (dx, dy, other) == (0, 0, 0):
                continue
            pl.semaphore_signal(
                barrier,
                inc=1,
                device_id={"member": (member + other) % 2, "tensor": peer(dx, dy)},
                device_id_type=pl.DeviceIdType.MESH,
            )
    for c in w_copy:
        c.start()

    small[0].wait()
    small[1].wait()
    slot = row * span + lax.broadcasted_iota(jnp.int32, (heads, span), 1)
    lane = lax.broadcasted_iota(jnp.int32, (heads, depth), 1)
    weights = []
    for r in range(rows):
        if r % half == 0:
            k_copy[r // half].wait()
        s = lax.dot_general(
            q_ref[r], k_ref[r], (((1,), (1,)), ((), ())), preferred_element_type=f32
        ) * (1.0 / depth**0.5)
        live = slot < len_ref[r]
        s = jnp.where(live, s, f32(-1e30))
        top = jnp.max(s, axis=-1, keepdims=True)
        w = jnp.where(live, jnp.exp(s - top), f32(0.0))
        total = jnp.sum(w, axis=-1, keepdims=True)
        weights.append(w.astype(bf16))
        att_send[pl.ds(rows + r, heads, stride=2 * rows), :] = jnp.where(
            lane < depth // 2, top, total
        )
    for c in v_copy:
        c.wait()
    for r in range(rows):
        att_send[pl.ds(r, heads, stride=2 * rows), :] = jnp.dot(
            weights[r], v_ref[r], preferred_element_type=f32
        )

    pl.semaphore_wait(barrier, 31)
    block = 4 * rows
    att_copy = []
    for dy in (2, 1, 3):
        to = (row + dy) % SIDE
        att_copy.append(
            pltpu.make_async_remote_copy(
                src_ref=att_send.at[pl.ds(pl.multiple_of(to * block, block), block), :],
                dst_ref=att_recv.at[SIDE - dy - 1],
                send_sem=att_ssem.at[dy - 1],
                recv_sem=att_rsem.at[SIDE - dy - 1],
                device_id={"tensor": col * SIDE + to},
                device_id_type=pl.DeviceIdType.MESH,
            )
        )
        att_copy[-1].start()
    small[3].wait()
    small[4].wait()
    mine = pl.ds(pl.multiple_of(me * width, width), width)
    side_copy = [
        pltpu.make_async_remote_copy(
            src_ref=src,
            dst_ref=dst,
            send_sem=side_ssem.at[i],
            recv_sem=side_rsem.at[i],
            device_id={"member": 1 - member},
            device_id_type=pl.DeviceIdType.MESH,
        )
        for i, (src, dst) in enumerate([(res_ref, res_other), (gain_ref.at[:, mine], gain_other)])
    ]
    for c in side_copy:
        c.start()
    inv_ref[...] = 1.0 / (gain_ref[...] * gain_ref[...])
    small[5].wait()
    small[2].wait()
    parts = [att_send[pl.ds(pl.multiple_of(row * block, block), block), :]]
    for c in att_copy:
        c.wait_recv()
    for i in range(SIDE - 1):
        parts.append(att_recv[i])
    attended = []
    for h in range(2):
        base = 2 * h * rows
        stats = [p[base + rows : base + 2 * rows] for p in parts]
        peak = functools.reduce(jnp.maximum, stats)
        num, den = 0.0, 0.0
        for p, st in zip(parts, stats):
            scale = jnp.exp(st - peak)[:, 0:1]
            num = num + scale * p[base : base + rows]
            den = den + scale * st[:, depth // 2 : depth // 2 + 1]
        attended.append(num / den)
    attended = jnp.concatenate(attended, axis=1).astype(bf16)

    def project(t):
        return jnp.dot(
            attended,
            wo_ref[:, pl.ds(pl.multiple_of(t * width, width), width)],
            preferred_element_type=f32,
        )

    rs_copy = []
    for dx, dy in OFFSETS + [(0, 0)]:
        t = peer(dx, dy)
        here, there = slot_of(dx, dy), slot_of(-dx, -dy)
        rs_send[here] = project(t).astype(bf16)
        rs_copy.append(
            pltpu.make_async_remote_copy(
                src_ref=rs_send.at[here],
                dst_ref=rs_recv.at[there],
                send_sem=rs_ssem.at[here],
                recv_sem=rs_rsem.at[there],
                device_id={"member": 1 - member, "tensor": t},
                device_id_type=pl.DeviceIdType.MESH,
            )
        )
        rs_copy[-1].start()
    for c in side_copy:
        c.wait_recv()
    hidden = res_other[...].astype(f32)
    for c in rs_copy[::-1]:
        c.wait_recv()
    for i in range(rs_recv.shape[0]):
        hidden = hidden + rs_recv[i].astype(f32)
    ag_ref[...] = (hidden * gain_other[...]).astype(bf16)
    ag_copy = {}
    for dx, dy in OFFSETS + [(0, 0)]:
        there = slot_of(-dx, -dy)
        ag_copy[there] = pltpu.make_async_remote_copy(
            src_ref=ag_ref,
            dst_ref=hg_ref.at[there],
            send_sem=ag_ssem.at[there],
            recv_sem=ag_rsem.at[there],
            device_id={"member": 1 - member, "tensor": peer(dx, dy)},
            device_id_type=pl.DeviceIdType.MESH,
        )
        ag_copy[there].start()

    for c in w_copy:
        c.wait()
    logits, square = 0.0, 0.0
    nearest = [(0, 0)] + OFFSETS[::-1]
    for i, (dx, dy) in enumerate(nearest):
        if i == 0 or hops(dx, dy) != hops(*nearest[i - 1]):
            for o in nearest:
                if hops(*o) == hops(dx, dy):
                    ag_copy[slot_of(*o)].wait_recv()
        t, k = peer(dx, dy), slot_of(dx, dy)
        here = pl.multiple_of(t * width, width)
        part = hg_ref[k]
        logits = logits + jnp.dot(part, wh_ref[pl.ds(here, width), :], preferred_element_type=f32)
        wide = part.astype(f32)
        square = square + wide * wide * inv_ref[:, pl.ds(here, width)]
    mean_square = jnp.sum(square, axis=-1, keepdims=True) * (1.0 / model)
    logits = logits * lax.rsqrt(mean_square + 1e-05)
    lg_ref[0] = logits[:half]
    lg_ref[1] = logits[half:]
    lg_copy = pltpu.make_async_remote_copy(
        src_ref=lg_ref.at[1 - member],
        dst_ref=lg_recv,
        send_sem=lg_ssem,
        recv_sem=lg_rsem,
        device_id={"member": 1 - member},
        device_id_type=pl.DeviceIdType.MESH,
    )
    lg_copy.start()

    vocab = logits.shape[1]
    ids = me * vocab + lax.broadcasted_iota(jnp.int32, (rows, vocab), 1)
    sub = lax.broadcasted_iota(jnp.int32, (rows, 1), 0)
    want = jnp.zeros((rows, 1), jnp.int32)
    for r in range(rows):
        want = jnp.where(sub == r, tgt_ref[r], want)
    pick = jnp.sum(jnp.where(ids == want, logits, f32(0.0)), axis=-1, keepdims=True)
    top = jnp.max(logits, axis=-1, keepdims=True)
    lse = top + jnp.log(jnp.sum(jnp.exp(logits - top), axis=-1, keepdims=True))
    lanes = lax.broadcasted_iota(jnp.int32, (rows, 128), 1)
    subs = lax.broadcasted_iota(jnp.int32, (rows, 128), 0)
    spread = jnp.where(lanes < 64, lse, pick)
    stat_ref[0] = jnp.sum(
        jnp.where(lanes // 8 % 8 == subs, spread, f32(0.0)), axis=0, keepdims=True
    )
    st_copy = []
    for dx, dy in OFFSETS + [(0, 0)]:
        for other in range(2):
            there = slot_of(-dx, -dy) + SIDE * SIDE * other
            if there == 0:
                continue
            st_copy.append(
                pltpu.make_async_remote_copy(
                    src_ref=stat_ref.at[0],
                    dst_ref=stat_ref.at[there],
                    send_sem=st_ssem.at[there - 1],
                    recv_sem=st_rsem.at[there - 1],
                    device_id={"member": (member + other) % 2, "tensor": peer(dx, dy)},
                    device_id_type=pl.DeviceIdType.MESH,
                )
            )
            st_copy[-1].start()
    lg_copy.wait_recv()
    mean_logits = 0.5 * (lg_ref[member] + lg_recv[...])
    for c in st_copy[::-1]:
        c.wait_recv()
    log_total, target = 0.0, 0.0
    for other in range(2):
        got = [stat_ref[other * SIDE * SIDE + i] for i in range(SIDE * SIDE)]
        peak = functools.reduce(jnp.maximum, got)
        log_total = log_total + 0.5 * (peak + jnp.log(sum(jnp.exp(g - peak) for g in got)))
        target = target + 0.5 * sum(got)
    lanes = lax.broadcasted_iota(jnp.int32, (half, 128), 1)
    mine = 8 * (member * half + lax.broadcasted_iota(jnp.int32, (half, 128), 0))
    shift = jnp.sum(jnp.where(lanes == mine, log_total, f32(0.0)), axis=-1, keepdims=True)
    chosen = jnp.sum(jnp.where(lanes == mine + 64, target, f32(0.0)), axis=-1, keepdims=True)
    out_ref[...] = mean_logits - shift
    tout_ref[...] = jnp.broadcast_to(chosen - shift, (half, 128))

    for c in att_copy + side_copy + rs_copy + list(ag_copy.values()) + [lg_copy] + st_copy:
        c.wait_send()


def local(queries, keys, values, lengths, targets, residual, out_weight, norm_gain, head_weight):
    rows, span, depth = keys.shape[1:]
    width, model = out_weight.shape[1:]
    vocab = head_weight.shape[2]
    peers = SIDE * SIDE - 1
    heads = HEADS // KV_HEADS
    f32, bf16 = jnp.float32, jnp.bfloat16
    dma = pltpu.SemaphoreType.DMA
    out, target = pl.pallas_call(
        step_kernel,
        out_shape=(
            jax.ShapeDtypeStruct((rows // 2, vocab), f32),
            jax.ShapeDtypeStruct((rows // 2, 128), f32),
        ),
        in_specs=[pl.BlockSpec(memory_space=HBM)] * 9,
        out_specs=(
            pl.BlockSpec(memory_space=pltpu.MemorySpace.VMEM),
            pl.BlockSpec(memory_space=pltpu.MemorySpace.VMEM),
        ),
        scratch_shapes=[
            pltpu.VMEM((rows, heads, depth), bf16),
            pltpu.VMEM((rows, span, depth), bf16),
            pltpu.VMEM((rows, span, depth), bf16),
            pltpu.SMEM((rows,), jnp.int32),
            pltpu.SMEM((rows,), jnp.int32),
            pltpu.VMEM((rows, width), bf16),
            pltpu.VMEM((width, model), bf16),
            pltpu.VMEM((1, model), f32),
            pltpu.VMEM((1, model), f32),
            pltpu.VMEM((model, vocab), bf16),
            pltpu.VMEM((rows, width), bf16),
            pltpu.VMEM((1, width), f32),
            pltpu.VMEM((2 * heads * rows, depth), f32),
            pltpu.VMEM((SIDE - 1, 4 * rows, depth), f32),
            pltpu.VMEM((peers + 1, rows, width), bf16),
            pltpu.VMEM((peers + 1, rows, width), bf16),
            pltpu.VMEM((rows, width), bf16),
            pltpu.VMEM((peers + 1, rows, width), bf16),
            pltpu.VMEM((2, rows // 2, vocab), f32),
            pltpu.VMEM((rows // 2, vocab), f32),
            pltpu.VMEM((2 * (peers + 1), 1, 128), f32),
            dma((6,)), dma((2,)), dma((2,)), dma((CHUNKS,)),
            dma((2,)), dma((2,)), dma((SIDE - 1,)), dma((SIDE - 1,)),
            dma((peers + 1,)), dma((peers + 1,)),
            dma((peers + 1,)), dma((peers + 1,)),
            dma, dma,
            dma((2 * peers + 1,)), dma((2 * peers + 1,)),
        ],
        compiler_params=pltpu.CompilerParams(
            collective_id=0, has_side_effects=True, vmem_limit_bytes=48 << 20
        ),
        name="decode_step",
    )(*(pltpu.with_memory_space_constraint(a, HBM) for a in (queries, keys, values, lengths, targets, residual, out_weight, norm_gain, head_weight)))
    return out, target[:, 0]


def solution(mesh):
    placed = (
        P("member", "rep", None, None),
        P("member", "rep", "tensor", None),
        P("member", "rep", "tensor", None),
        P("rep"),
        P("rep"),
        P("member", "rep", None),
        P("member", "tensor", None),
        P("member", None),
        P("member", None, "tensor"),
    )
    return jax.shard_map(
        local,
        mesh=mesh,
        in_specs=placed,
        out_specs=(P(("rep", "member"), "tensor"), P(("rep", "member"))),
        check_vma=False,
    )
```

```python
import functools

import jax
import jax.numpy as jnp
from jax import lax
from jax.experimental import pallas as pl
from jax.experimental.pallas import tpu as pltpu
from jax.sharding import PartitionSpec as P

HEADS = 32
KV_HEADS = 4
SIDE = 4
CHUNKS = 4
HBM = pltpu.MemorySpace.HBM


def hops(dx, dy):
    return min(dx, SIDE - dx) + min(dy, SIDE - dy)


OFFSETS = sorted(
    [(dx, dy) for dx in range(SIDE) for dy in range(SIDE) if (dx, dy) != (0, 0)],
    key=lambda o: -hops(*o),
)


NEAREST = [(0, 0)] + OFFSETS[::-1]
SLOT = {o: i for i, o in enumerate(NEAREST)}
REACH = [[i for i, o in enumerate(NEAREST) if hops(*o) == n] for n in range(SIDE + 1)]


def slot_of(dx, dy):
    return SLOT[dx % SIDE, dy % SIDE]


def arrival(ref, sem):
    return pltpu.make_async_copy(ref, ref, sem)


def step_kernel(
    q_hbm, k_hbm, v_hbm, len_hbm, tgt_hbm, res_hbm, wo_hbm, gain_hbm, wh_hbm,
    out_ref, tout_ref,
    q_ref, k_ref, v_ref, len_ref, tgt_ref, res_ref, wo_ref, gain_ref, inv_ref, wh_ref,
    res_other, gain_other, att_send, att_recv, rs_send, rs_recv, ag_ref, hg_ref, lg_ref, lg_recv, stat_ref,
    in_sem, k_sem, v_sem, wh_sem,
    side_ssem, side_rsem, att_ssem, att_rsem, rs_ssem, rs_rsem, ag_ssem, ag_rsem, lg_ssem, lg_rsem, st_ssem, st_rsem,
):
    me = lax.axis_index("tensor")
    member = lax.axis_index("member")
    col, row = me // SIDE, me % SIDE
    rows, span, depth = k_ref.shape
    heads = HEADS // KV_HEADS
    width = wo_ref.shape[0]
    f32, bf16 = jnp.float32, jnp.bfloat16

    def peer(dx, dy):
        return (col + dx) % SIDE * SIDE + (row + dy) % SIDE

    small = [
        pltpu.make_async_copy(q_hbm.at[0, :, pl.ds(col * heads, heads), :], q_ref, in_sem.at[0]),
        pltpu.make_async_copy(len_hbm, len_ref, in_sem.at[1]),
        pltpu.make_async_copy(tgt_hbm, tgt_ref, in_sem.at[2]),
        pltpu.make_async_copy(
            res_hbm.at[0, :, pl.ds(pl.multiple_of(me * width, width), width)], res_ref, in_sem.at[3]
        ),
        pltpu.make_async_copy(gain_hbm, gain_ref, in_sem.at[4]),
        pltpu.make_async_copy(wo_hbm.at[0], wo_ref, in_sem.at[5]),
    ]
    half = rows // 2
    k_copy = pltpu.make_async_copy(k_hbm.at[0], k_ref, k_sem)
    v_copy = pltpu.make_async_copy(v_hbm.at[0], v_ref, v_sem)
    model = wh_ref.shape[0]
    chunk = model // CHUNKS
    w_copy = [
        pltpu.make_async_copy(
            wh_hbm.at[0, pl.ds(c * chunk, chunk), :], wh_ref.at[pl.ds(c * chunk, chunk), :], wh_sem
        )
        for c in range(CHUNKS)
    ]
    small[0].start()
    small[1].start()
    k_copy.start()
    v_copy.start()
    barrier = pltpu.get_barrier_semaphore()
    near = [o for o in OFFSETS + [(0, 0)] if 0 in o]
    for dx, dy in near:
        for other in range(2):
            if (dx, dy, other) == (0, 0, 0):
                continue
            pl.semaphore_signal(
                barrier,
                inc=1,
                device_id={"member": (member + other) % 2, "tensor": peer(dx, dy)},
                device_id_type=pl.DeviceIdType.MESH,
            )
    for c in small[2:] + w_copy:
        c.start()

    small[0].wait()
    small[1].wait()
    k_copy.wait()
    slot = row * span + lax.broadcasted_iota(jnp.int32, (heads, span), 1)
    lane = lax.broadcasted_iota(jnp.int32, (heads, depth), 1)
    weights = []
    for r in range(rows):
        s = lax.dot_general(
            q_ref[r], k_ref[r], (((1,), (1,)), ((), ())), preferred_element_type=f32
        ) * (1.0 / depth**0.5)
        live = slot < len_ref[r]
        s = jnp.where(live, s, f32(-1e30))
        top = jnp.max(s, axis=-1, keepdims=True)
        w = jnp.where(live, jnp.exp(s - top), f32(0.0))
        total = jnp.sum(w, axis=-1, keepdims=True)
        weights.append(w.astype(bf16))
        att_send[pl.ds(rows + r, heads, stride=2 * rows), :] = jnp.where(
            lane < depth // 2, top, total
        )
    v_copy.wait()
    for r in range(rows):
        att_send[pl.ds(r, heads, stride=2 * rows), :] = jnp.dot(
            weights[r], v_ref[r], preferred_element_type=f32
        )

    pl.semaphore_wait(barrier, 2 * len(near) - 1)
    block = 4 * rows
    for dy in (2, 1, 3):
        to = (row + dy) % SIDE
        pltpu.make_async_remote_copy(
            src_ref=att_send.at[pl.ds(pl.multiple_of(to * block, block), block), :],
            dst_ref=att_recv.at[SIDE - dy - 1],
            send_sem=att_ssem,
            recv_sem=att_rsem,
            device_id={"tensor": col * SIDE + to},
            device_id_type=pl.DeviceIdType.MESH,
        ).start()
    small[3].wait()
    small[4].wait()
    mine = pl.ds(pl.multiple_of(me * width, width), width)
    side_copy = [
        pltpu.make_async_remote_copy(
            src_ref=src,
            dst_ref=dst,
            send_sem=side_ssem.at[i],
            recv_sem=side_rsem.at[i],
            device_id={"member": 1 - member},
            device_id_type=pl.DeviceIdType.MESH,
        )
        for i, (src, dst) in enumerate([(res_ref, res_other), (gain_ref.at[:, mine], gain_other)])
    ]
    for c in side_copy:
        c.start()
    inv_ref[...] = 1.0 / (gain_ref[...] * gain_ref[...])
    small[5].wait()
    small[2].wait()
    parts = [att_send[pl.ds(pl.multiple_of(row * block, block), block), :]]
    arrival(att_recv, att_rsem).wait()
    for i in range(SIDE - 1):
        parts.append(att_recv[i])
    attended = []
    for h in range(2):
        base = 2 * h * rows
        stats = [p[base + rows : base + 2 * rows] for p in parts]
        peak = functools.reduce(jnp.maximum, stats)
        num, den = 0.0, 0.0
        for p, st in zip(parts, stats):
            scale = jnp.exp(st - peak)[:, 0:1]
            num = num + scale * p[base : base + rows]
            den = den + scale * st[:, depth // 2 : depth // 2 + 1]
        attended.append(num / den)
    attended = jnp.concatenate(attended, axis=1).astype(bf16)

    def project(t):
        return jnp.dot(
            attended,
            wo_ref[:, pl.ds(pl.multiple_of(t * width, width), width)],
            preferred_element_type=f32,
        )

    for dx, dy in OFFSETS + [(0, 0)]:
        t = peer(dx, dy)
        here, there = slot_of(dx, dy), slot_of(-dx, -dy)
        rs_send[here] = project(t).astype(bf16)
        pltpu.make_async_remote_copy(
            src_ref=rs_send.at[here],
            dst_ref=rs_recv.at[there],
            send_sem=rs_ssem,
            recv_sem=rs_rsem,
            device_id={"member": 1 - member, "tensor": t},
            device_id_type=pl.DeviceIdType.MESH,
        ).start()
    for c in side_copy:
        c.wait_recv()
    hidden = res_other[...].astype(f32)
    arrival(rs_recv, rs_rsem).wait()
    for i in range(rs_recv.shape[0]):
        hidden = hidden + rs_recv[i].astype(f32)
    ag_ref[...] = (hidden * gain_other[...]).astype(bf16)
    for dx, dy in OFFSETS + [(0, 0)]:
        there = slot_of(-dx, -dy)
        pltpu.make_async_remote_copy(
            src_ref=ag_ref,
            dst_ref=hg_ref.at[there],
            send_sem=ag_ssem,
            recv_sem=ag_rsem.at[hops(dx, dy)],
            device_id={"member": 1 - member, "tensor": peer(dx, dy)},
            device_id_type=pl.DeviceIdType.MESH,
        ).start()

    arrival(wh_ref, wh_sem).wait()
    logits, square = 0.0, 0.0
    for k, (dx, dy) in enumerate(NEAREST):
        group = REACH[hops(dx, dy)]
        if k == group[0]:
            arrival(hg_ref.at[pl.ds(k, len(group))], ag_rsem.at[hops(dx, dy)]).wait()
        t = peer(dx, dy)
        here = pl.multiple_of(t * width, width)
        part = hg_ref[k]
        logits = logits + jnp.dot(part, wh_ref[pl.ds(here, width), :], preferred_element_type=f32)
        wide = part.astype(f32)
        square = square + wide * wide * inv_ref[:, pl.ds(here, width)]
    mean_square = jnp.sum(square, axis=-1, keepdims=True) * (1.0 / model)
    logits = logits * lax.rsqrt(mean_square + 1e-05)
    lg_ref[0] = logits[:half]
    lg_ref[1] = logits[half:]
    lg_copy = pltpu.make_async_remote_copy(
        src_ref=lg_ref.at[1 - member],
        dst_ref=lg_recv,
        send_sem=lg_ssem,
        recv_sem=lg_rsem,
        device_id={"member": 1 - member},
        device_id_type=pl.DeviceIdType.MESH,
    )
    lg_copy.start()

    vocab = logits.shape[1]
    ids = me * vocab + lax.broadcasted_iota(jnp.int32, (rows, vocab), 1)
    sub = lax.broadcasted_iota(jnp.int32, (rows, 1), 0)
    want = jnp.zeros((rows, 1), jnp.int32)
    for r in range(rows):
        want = jnp.where(sub == r, tgt_ref[r], want)
    pick = jnp.sum(jnp.where(ids == want, logits, f32(0.0)), axis=-1, keepdims=True)
    top = jnp.max(logits, axis=-1, keepdims=True)
    lse = top + jnp.log(jnp.sum(jnp.exp(logits - top), axis=-1, keepdims=True))
    lanes = lax.broadcasted_iota(jnp.int32, (rows, 128), 1)
    subs = lax.broadcasted_iota(jnp.int32, (rows, 128), 0)
    spread = jnp.where(lanes < 64, lse, pick)
    stat_ref[0] = jnp.sum(
        jnp.where(lanes // 8 % 8 == subs, spread, f32(0.0)), axis=0, keepdims=True
    )
    for dx, dy in OFFSETS + [(0, 0)]:
        for other in range(2):
            there = slot_of(-dx, -dy) + SIDE * SIDE * other
            if there == 0:
                continue
            pltpu.make_async_remote_copy(
                src_ref=stat_ref.at[0],
                dst_ref=stat_ref.at[there],
                send_sem=st_ssem,
                recv_sem=st_rsem,
                device_id={"member": (member + other) % 2, "tensor": peer(dx, dy)},
                device_id_type=pl.DeviceIdType.MESH,
            ).start()
    lg_copy.wait_recv()
    mean_logits = 0.5 * (lg_ref[member] + lg_recv[...])
    got_stats = stat_ref.at[pl.ds(1, stat_ref.shape[0] - 1)]
    arrival(got_stats, st_rsem).wait()
    log_total, target = 0.0, 0.0
    for other in range(2):
        got = [stat_ref[other * SIDE * SIDE + i] for i in range(SIDE * SIDE)]
        peak = functools.reduce(jnp.maximum, got)
        log_total = log_total + 0.5 * (peak + jnp.log(sum(jnp.exp(g - peak) for g in got)))
        target = target + 0.5 * sum(got)
    lanes = lax.broadcasted_iota(jnp.int32, (half, 128), 1)
    mine = 8 * (member * half + lax.broadcasted_iota(jnp.int32, (half, 128), 0))
    shift = jnp.sum(jnp.where(lanes == mine, log_total, f32(0.0)), axis=-1, keepdims=True)
    chosen = jnp.sum(jnp.where(lanes == mine + 64, target, f32(0.0)), axis=-1, keepdims=True)
    out_ref[...] = mean_logits - shift
    tout_ref[...] = jnp.broadcast_to(chosen - shift, (half, 128))

    arrival(att_recv, att_ssem).wait()
    arrival(rs_send, rs_ssem).wait()
    arrival(hg_ref, ag_ssem).wait()
    arrival(got_stats, st_ssem).wait()
    for c in side_copy + [lg_copy]:
        c.wait_send()


def local(queries, keys, values, lengths, targets, residual, out_weight, norm_gain, head_weight):
    rows, span, depth = keys.shape[1:]
    width, model = out_weight.shape[1:]
    vocab = head_weight.shape[2]
    peers = SIDE * SIDE - 1
    heads = HEADS // KV_HEADS
    f32, bf16 = jnp.float32, jnp.bfloat16
    dma = pltpu.SemaphoreType.DMA
    out, target = pl.pallas_call(
        step_kernel,
        out_shape=(
            jax.ShapeDtypeStruct((rows // 2, vocab), f32),
            jax.ShapeDtypeStruct((rows // 2, 128), f32),
        ),
        in_specs=[pl.BlockSpec(memory_space=HBM)] * 9,
        out_specs=(
            pl.BlockSpec(memory_space=pltpu.MemorySpace.VMEM),
            pl.BlockSpec(memory_space=pltpu.MemorySpace.VMEM),
        ),
        scratch_shapes=[
            pltpu.VMEM((rows, heads, depth), bf16),
            pltpu.VMEM((rows, span, depth), bf16),
            pltpu.VMEM((rows, span, depth), bf16),
            pltpu.SMEM((rows,), jnp.int32),
            pltpu.SMEM((rows,), jnp.int32),
            pltpu.VMEM((rows, width), bf16),
            pltpu.VMEM((width, model), bf16),
            pltpu.VMEM((1, model), f32),
            pltpu.VMEM((1, model), f32),
            pltpu.VMEM((model, vocab), bf16),
            pltpu.VMEM((rows, width), bf16),
            pltpu.VMEM((1, width), f32),
            pltpu.VMEM((2 * heads * rows, depth), f32),
            pltpu.VMEM((SIDE - 1, 4 * rows, depth), f32),
            pltpu.VMEM((peers + 1, rows, width), bf16),
            pltpu.VMEM((peers + 1, rows, width), bf16),
            pltpu.VMEM((rows, width), bf16),
            pltpu.VMEM((peers + 1, rows, width), bf16),
            pltpu.VMEM((2, rows // 2, vocab), f32),
            pltpu.VMEM((rows // 2, vocab), f32),
            pltpu.VMEM((2 * (peers + 1), 1, 128), f32),
            dma((6,)), dma, dma, dma,
            dma((2,)), dma((2,)), dma, dma,
            dma, dma,
            dma, dma((SIDE + 1,)),
            dma, dma,
            dma, dma,
        ],
        compiler_params=pltpu.CompilerParams(
            collective_id=0, has_side_effects=True, vmem_limit_bytes=48 << 20
        ),
        name="decode_step",
    )(*(pltpu.with_memory_space_constraint(a, HBM) for a in (queries, keys, values, lengths, targets, residual, out_weight, norm_gain, head_weight)))
    return out, target[:, 0]


def solution(mesh):
    placed = (
        P("member", "rep", None, None),
        P("member", "rep", "tensor", None),
        P("member", "rep", "tensor", None),
        P("rep"),
        P("rep"),
        P("member", "rep", None),
        P("member", "tensor", None),
        P("member", None),
        P("member", None, "tensor"),
    )
    return jax.shard_map(
        local,
        mesh=mesh,
        in_specs=placed,
        out_specs=(P(("rep", "member"), "tensor"), P(("rep", "member"))),
        check_vma=False,
    )
```

```python
import functools

import jax
import jax.numpy as jnp
from jax import lax
from jax.experimental import pallas as pl
from jax.experimental.pallas import tpu as pltpu
from jax.sharding import PartitionSpec as P

HEADS = 32
KV_HEADS = 4
SIDE = 4
CHUNKS = 4
HBM = pltpu.MemorySpace.HBM


def hops(dx, dy):
    return min(dx, SIDE - dx) + min(dy, SIDE - dy)


OFFSETS = sorted(
    [(dx, dy) for dx in range(SIDE) for dy in range(SIDE) if (dx, dy) != (0, 0)],
    key=lambda o: -hops(*o),
)


NEAREST = [(0, 0)] + OFFSETS[::-1]
SLOT = {o: i for i, o in enumerate(NEAREST)}
REACH = [[i for i, o in enumerate(NEAREST) if hops(*o) == n] for n in range(SIDE + 1)]


def slot_of(dx, dy):
    return SLOT[dx % SIDE, dy % SIDE]


def arrival(ref, sem):
    return pltpu.make_async_copy(ref, ref, sem)


def step_kernel(
    q_hbm, k_hbm, v_hbm, len_hbm, tgt_hbm, res_hbm, wo_hbm, gain_hbm, wh_hbm,
    out_ref, tout_ref,
    q_ref, k_ref, v_ref, len_ref, tgt_ref, res_ref, wo_ref, gain_ref, inv_ref, wh_ref,
    res_other, gain_other, att_send, att_recv, rs_send, rs_recv, ag_ref, hg_ref, lg_ref, lg_recv, stat_ref,
    in_sem, k_sem, v_sem, wh_sem,
    side_ssem, side_rsem, att_ssem, att_rsem, rs_ssem, rs_rsem, ag_ssem, ag_rsem, lg_ssem, lg_rsem, st_ssem, st_rsem,
):
    me = lax.axis_index("tensor")
    member = lax.axis_index("member")
    col, row = me // SIDE, me % SIDE
    rows, span, depth = k_ref.shape
    heads = HEADS // KV_HEADS
    width = wo_ref.shape[0]
    f32, bf16 = jnp.float32, jnp.bfloat16

    def peer(dx, dy):
        return (col + dx) % SIDE * SIDE + (row + dy) % SIDE

    small = [
        pltpu.make_async_copy(q_hbm.at[0, :, pl.ds(col * heads, heads), :], q_ref, in_sem.at[0]),
        pltpu.make_async_copy(len_hbm, len_ref, in_sem.at[1]),
        pltpu.make_async_copy(tgt_hbm, tgt_ref, in_sem.at[2]),
        pltpu.make_async_copy(
            res_hbm.at[0, :, pl.ds(pl.multiple_of(me * width, width), width)], res_ref, in_sem.at[3]
        ),
        pltpu.make_async_copy(gain_hbm, gain_ref, in_sem.at[4]),
        pltpu.make_async_copy(wo_hbm.at[0], wo_ref, in_sem.at[5]),
    ]
    half = rows // 2
    k_copy = pltpu.make_async_copy(k_hbm.at[0], k_ref, k_sem)
    v_copy = pltpu.make_async_copy(v_hbm.at[0], v_ref, v_sem)
    model = wh_ref.shape[0]
    chunk = model // CHUNKS
    w_copy = [
        pltpu.make_async_copy(
            wh_hbm.at[0, pl.ds(c * chunk, chunk), :], wh_ref.at[pl.ds(c * chunk, chunk), :], wh_sem
        )
        for c in range(CHUNKS)
    ]
    small[0].start()
    small[1].start()
    k_copy.start()
    v_copy.start()
    barrier = pltpu.get_barrier_semaphore()
    near = [o for o in OFFSETS + [(0, 0)] if 0 in o]
    for dx, dy in near:
        for other in range(2):
            if (dx, dy, other) == (0, 0, 0):
                continue
            pl.semaphore_signal(
                barrier,
                inc=1,
                device_id={"member": (member + other) % 2, "tensor": peer(dx, dy)},
                device_id_type=pl.DeviceIdType.MESH,
            )
    for c in small[2:] + w_copy:
        c.start()

    small[0].wait()
    small[1].wait()
    k_copy.wait()
    slot = row * span + lax.broadcasted_iota(jnp.int32, (heads, span), 1)
    lane = lax.broadcasted_iota(jnp.int32, (heads, depth), 1)
    weights = []
    for r in range(rows):
        s = lax.dot_general(
            q_ref[r], k_ref[r], (((1,), (1,)), ((), ())), preferred_element_type=f32
        ) * (1.0 / depth**0.5)
        live = slot < len_ref[r]
        s = jnp.where(live, s, f32(-1e30))
        top = jnp.max(s, axis=-1, keepdims=True)
        w = jnp.where(live, jnp.exp(s - top), f32(0.0))
        total = jnp.sum(w, axis=-1, keepdims=True)
        weights.append(w.astype(bf16))
        att_send[pl.ds(rows + r, heads, stride=2 * rows), :] = jnp.where(
            lane < depth // 2, top, total
        )
    v_copy.wait()
    for r in range(rows):
        att_send[pl.ds(r, heads, stride=2 * rows), :] = jnp.dot(
            weights[r], v_ref[r], preferred_element_type=f32
        )

    pl.semaphore_wait(barrier, 2 * len(near) - 1)
    block = 4 * rows
    for dy in (2, 1, 3):
        to = (row + dy) % SIDE
        pltpu.make_async_remote_copy(
            src_ref=att_send.at[pl.ds(pl.multiple_of(to * block, block), block), :],
            dst_ref=att_recv.at[SIDE - dy - 1],
            send_sem=att_ssem,
            recv_sem=att_rsem,
            device_id={"tensor": col * SIDE + to},
            device_id_type=pl.DeviceIdType.MESH,
        ).start()
    small[3].wait()
    small[4].wait()
    mine = pl.ds(pl.multiple_of(me * width, width), width)
    side_copy = [
        pltpu.make_async_remote_copy(
            src_ref=src,
            dst_ref=dst,
            send_sem=side_ssem.at[i],
            recv_sem=side_rsem.at[i],
            device_id={"member": 1 - member},
            device_id_type=pl.DeviceIdType.MESH,
        )
        for i, (src, dst) in enumerate([(res_ref, res_other), (gain_ref.at[:, mine], gain_other)])
    ]
    for c in side_copy:
        c.start()
    inv_ref[...] = 1.0 / (gain_ref[...] * gain_ref[...])
    small[5].wait()
    small[2].wait()
    parts = [att_send[pl.ds(pl.multiple_of(row * block, block), block), :]]
    arrival(att_recv, att_rsem).wait()
    for i in range(SIDE - 1):
        parts.append(att_recv[i])
    attended = []
    for h in range(2):
        base = 2 * h * rows
        stats = [p[base + rows : base + 2 * rows] for p in parts]
        peak = functools.reduce(jnp.maximum, stats)
        num, den = 0.0, 0.0
        for p, st in zip(parts, stats):
            scale = jnp.exp(st - peak)[:, 0:1]
            num = num + scale * p[base : base + rows]
            den = den + scale * st[:, depth // 2 : depth // 2 + 1]
        attended.append(num / den)
    attended = jnp.concatenate(attended, axis=1).astype(bf16)

    def project(t):
        return jnp.dot(
            attended,
            wo_ref[:, pl.ds(pl.multiple_of(t * width, width), width)],
            preferred_element_type=f32,
        )

    for dx, dy in OFFSETS + [(0, 0)]:
        t = peer(dx, dy)
        here, there = slot_of(dx, dy), slot_of(-dx, -dy)
        rs_send[here] = project(t).astype(bf16)
        pltpu.make_async_remote_copy(
            src_ref=rs_send.at[here],
            dst_ref=rs_recv.at[there],
            send_sem=rs_ssem,
            recv_sem=rs_rsem,
            device_id={"member": 1 - member, "tensor": t},
            device_id_type=pl.DeviceIdType.MESH,
        ).start()
    for c in side_copy:
        c.wait_recv()
    hidden = res_other[...].astype(f32)
    arrival(rs_recv, rs_rsem).wait()
    for i in range(rs_recv.shape[0]):
        hidden = hidden + rs_recv[i].astype(f32)
    ag_ref[...] = (hidden * gain_other[...]).astype(bf16)
    for dx, dy in OFFSETS + [(0, 0)]:
        there = slot_of(-dx, -dy)
        pltpu.make_async_remote_copy(
            src_ref=ag_ref,
            dst_ref=hg_ref.at[there],
            send_sem=ag_ssem,
            recv_sem=ag_rsem.at[hops(dx, dy)],
            device_id={"member": 1 - member, "tensor": peer(dx, dy)},
            device_id_type=pl.DeviceIdType.MESH,
        ).start()

    arrival(wh_ref, wh_sem).wait()
    logits, square = 0.0, 0.0
    for k, (dx, dy) in enumerate(NEAREST):
        group = REACH[hops(dx, dy)]
        if k == group[0]:
            arrival(hg_ref.at[pl.ds(k, len(group))], ag_rsem.at[hops(dx, dy)]).wait()
        t = peer(dx, dy)
        here = pl.multiple_of(t * width, width)
        part = hg_ref[k]
        logits = logits + jnp.dot(part, wh_ref[pl.ds(here, width), :], preferred_element_type=f32)
        wide = part.astype(f32)
        square = square + wide * wide * inv_ref[:, pl.ds(here, width)]
    mean_square = jnp.sum(square, axis=-1, keepdims=True) * (1.0 / model)
    logits = logits * lax.rsqrt(mean_square + 1e-05)
    lg_ref[0] = logits[:half]
    lg_ref[1] = logits[half:]
    lg_copy = pltpu.make_async_remote_copy(
        src_ref=lg_ref.at[1 - member],
        dst_ref=lg_recv,
        send_sem=lg_ssem,
        recv_sem=lg_rsem,
        device_id={"member": 1 - member},
        device_id_type=pl.DeviceIdType.MESH,
    )
    lg_copy.start()

    vocab = logits.shape[1]
    ids = me * vocab + lax.broadcasted_iota(jnp.int32, (rows, vocab), 1)
    sub = lax.broadcasted_iota(jnp.int32, (rows, 1), 0)
    want = jnp.zeros((rows, 1), jnp.int32)
    for r in range(rows):
        want = jnp.where(sub == r, tgt_ref[r], want)
    pick = jnp.sum(jnp.where(ids == want, logits, f32(0.0)), axis=-1, keepdims=True)
    top = jnp.max(logits, axis=-1, keepdims=True)
    lse = top + jnp.log(jnp.sum(jnp.exp(logits - top), axis=-1, keepdims=True))
    lanes = lax.broadcasted_iota(jnp.int32, (rows, 128), 1)
    subs = lax.broadcasted_iota(jnp.int32, (rows, 128), 0)
    spread = jnp.where(lanes < 64, lse, pick)
    stat_ref[0:1] = jnp.sum(
        jnp.where(lanes // 8 % 8 == subs, spread, f32(0.0)), axis=0, keepdims=True
    )
    for dx, dy in OFFSETS + [(0, 0)]:
        for other in range(2):
            there = slot_of(-dx, -dy) + SIDE * SIDE * other
            if there == 0:
                continue
            pltpu.make_async_remote_copy(
                src_ref=stat_ref.at[0:1],
                dst_ref=stat_ref.at[there : there + 1],
                send_sem=st_ssem,
                recv_sem=st_rsem,
                device_id={"member": (member + other) % 2, "tensor": peer(dx, dy)},
                device_id_type=pl.DeviceIdType.MESH,
            ).start()
    lg_copy.wait_recv()
    mean_logits = 0.5 * (lg_ref[member] + lg_recv[...])
    got_stats = stat_ref.at[pl.ds(1, stat_ref.shape[0] - 1)]
    arrival(got_stats, st_rsem).wait()
    log_total, target = 0.0, 0.0
    for other in range(2):
        got = stat_ref[other * SIDE * SIDE : (other + 1) * SIDE * SIDE]
        peak = jnp.max(got, axis=0, keepdims=True)
        total = jnp.sum(jnp.exp(got - peak), axis=0, keepdims=True)
        log_total = log_total + 0.5 * (peak + jnp.log(total))
        target = target + 0.5 * jnp.sum(got, axis=0, keepdims=True)
    lanes = lax.broadcasted_iota(jnp.int32, (half, 128), 1)
    mine = 8 * (member * half + lax.broadcasted_iota(jnp.int32, (half, 128), 0))
    shift = jnp.sum(jnp.where(lanes == mine, log_total, f32(0.0)), axis=-1, keepdims=True)
    chosen = jnp.sum(jnp.where(lanes == mine + 64, target, f32(0.0)), axis=-1, keepdims=True)
    out_ref[...] = mean_logits - shift
    tout_ref[...] = (chosen - shift)[:, 0]

    arrival(att_recv, att_ssem).wait()
    arrival(rs_send, rs_ssem).wait()
    arrival(hg_ref, ag_ssem).wait()
    arrival(got_stats, st_ssem).wait()
    for c in side_copy + [lg_copy]:
        c.wait_send()


def write_out(out_ref, target_ref, out_hbm, target_hbm, out_sem, target_sem):
    copies = [
        pltpu.make_async_copy(out_ref, out_hbm, out_sem),
        pltpu.make_async_copy(target_ref, target_hbm, target_sem),
    ]
    for c in copies:
        c.start()
    for c in copies:
        c.wait()


def local(queries, keys, values, lengths, targets, residual, out_weight, norm_gain, head_weight):
    rows, span, depth = keys.shape[1:]
    width, model = out_weight.shape[1:]
    vocab = head_weight.shape[2]
    peers = SIDE * SIDE - 1
    heads = HEADS // KV_HEADS
    f32, bf16 = jnp.float32, jnp.bfloat16
    dma = pltpu.SemaphoreType.DMA
    out, target = pl.pallas_call(
        step_kernel,
        out_shape=(
            jax.ShapeDtypeStruct((rows // 2, vocab), f32),
            jax.ShapeDtypeStruct((rows // 2,), f32),
        ),
        in_specs=[pl.BlockSpec(memory_space=HBM)] * 9,
        out_specs=(
            pl.BlockSpec(memory_space=pltpu.MemorySpace.VMEM),
            pl.BlockSpec(memory_space=pltpu.MemorySpace.VMEM),
        ),
        scratch_shapes=[
            pltpu.VMEM((rows, heads, depth), bf16),
            pltpu.VMEM((rows, span, depth), bf16),
            pltpu.VMEM((rows, span, depth), bf16),
            pltpu.SMEM((rows,), jnp.int32),
            pltpu.SMEM((rows,), jnp.int32),
            pltpu.VMEM((rows, width), bf16),
            pltpu.VMEM((width, model), bf16),
            pltpu.VMEM((1, model), f32),
            pltpu.VMEM((1, model), f32),
            pltpu.VMEM((model, vocab), bf16),
            pltpu.VMEM((rows, width), bf16),
            pltpu.VMEM((1, width), f32),
            pltpu.VMEM((2 * heads * rows, depth), f32),
            pltpu.VMEM((SIDE - 1, 4 * rows, depth), f32),
            pltpu.VMEM((peers + 1, rows, width), bf16),
            pltpu.VMEM((peers + 1, rows, width), bf16),
            pltpu.VMEM((rows, width), bf16),
            pltpu.VMEM((peers + 1, rows, width), bf16),
            pltpu.VMEM((2, rows // 2, vocab), f32),
            pltpu.VMEM((rows // 2, vocab), f32),
            pltpu.VMEM((2 * (peers + 1), 128), f32),
            dma((6,)), dma, dma, dma,
            dma((2,)), dma((2,)), dma, dma,
            dma, dma,
            dma, dma((SIDE + 1,)),
            dma, dma,
            dma, dma,
        ],
        compiler_params=pltpu.CompilerParams(
            collective_id=0, has_side_effects=True, vmem_limit_bytes=48 << 20
        ),
        name="decode_step",
    )(*(pltpu.with_memory_space_constraint(a, HBM) for a in (queries, keys, values, lengths, targets, residual, out_weight, norm_gain, head_weight)))
    return pl.pallas_call(
        write_out,
        out_shape=(
            jax.ShapeDtypeStruct((rows // 2, vocab), f32),
            jax.ShapeDtypeStruct((rows // 2,), f32),
        ),
        in_specs=[pl.BlockSpec(memory_space=pltpu.MemorySpace.VMEM)] * 2,
        out_specs=(pl.BlockSpec(memory_space=HBM), pl.BlockSpec(memory_space=HBM)),
        scratch_shapes=[dma, dma],
        compiler_params=pltpu.CompilerParams(vmem_limit_bytes=1 << 20),
        name="write_out",
    )(out, target)


def solution(mesh):
    placed = (
        P("member", "rep", None, None),
        P("member", "rep", "tensor", None),
        P("member", "rep", "tensor", None),
        P("rep"),
        P("rep"),
        P("member", "rep", None),
        P("member", "tensor", None),
        P("member", None),
        P("member", None, "tensor"),
    )
    return jax.shard_map(
        local,
        mesh=mesh,
        in_specs=placed,
        out_specs=(P(("rep", "member"), "tensor"), P(("rep", "member"))),
        check_vma=False,
    )
```

```python
import functools

import jax
import jax.numpy as jnp
from jax import lax
from jax.experimental import pallas as pl
from jax.experimental.pallas import tpu as pltpu
from jax.sharding import PartitionSpec as P

HEADS = 32
KV_HEADS = 4
SIDE = 4
CHUNKS = 4
HBM = pltpu.MemorySpace.HBM


def hops(dx, dy):
    return min(dx, SIDE - dx) + min(dy, SIDE - dy)


OFFSETS = sorted(
    [(dx, dy) for dx in range(SIDE) for dy in range(SIDE) if (dx, dy) != (0, 0)],
    key=lambda o: -hops(*o),
)


NEAREST = [(0, 0)] + OFFSETS[::-1]
SLOT = {o: i for i, o in enumerate(NEAREST)}
REACH = [[i for i, o in enumerate(NEAREST) if hops(*o) == n] for n in range(SIDE + 1)]


def slot_of(dx, dy):
    return SLOT[dx % SIDE, dy % SIDE]


def arrival(ref, sem):
    return pltpu.make_async_copy(ref, ref, sem)


def step_kernel(
    q_hbm, k_hbm, v_hbm, len_hbm, tgt_hbm, res_hbm, wo_hbm, gain_hbm, wh_hbm,
    out_ref, tout_ref,
    q_ref, k_ref, v_ref, len_ref, tgt_ref, res_ref, wo_ref, gain_ref, inv_ref, wh_ref,
    res_other, gain_mine, gain_other, att_send, att_recv, rs_send, rs_recv, ag_ref, hg_near, hg_mid, lg_ref, lg_recv, stat_ref,
    in_sem, k_sem, v_sem, wh_sem,
    side_ssem, side_rsem, att_ssem, att_rsem, rs_ssem, rs_rsem, ag_ssem, ag_rsem, lg_ssem, lg_rsem, st_ssem, st_rsem,
):
    me = lax.axis_index("tensor")
    member = lax.axis_index("member")
    col, row = me // SIDE, me % SIDE
    rows, span, depth = k_ref.shape
    heads = HEADS // KV_HEADS
    width = wo_ref.shape[0]
    f32, bf16 = jnp.float32, jnp.bfloat16

    def peer(dx, dy):
        return (col + dx) % SIDE * SIDE + (row + dy) % SIDE

    def columns(t):
        return pl.ds(pl.multiple_of(t * width, width), width)

    small = [
        pltpu.make_async_copy(q_hbm.at[0, :, pl.ds(col * heads, heads), :], q_ref, in_sem.at[0]),
        pltpu.make_async_copy(len_hbm, len_ref, in_sem.at[1]),
        pltpu.make_async_copy(tgt_hbm, tgt_ref, in_sem.at[2]),
        pltpu.make_async_copy(res_hbm.at[0, :, columns(me)], res_ref.at[0], in_sem.at[3]),
        pltpu.make_async_copy(gain_hbm, gain_ref, in_sem.at[4]),
        pltpu.make_async_copy(wo_hbm.at[0], wo_ref, in_sem.at[5]),
        pltpu.make_async_copy(res_hbm.at[0, :, columns(peer(2, 2))], res_ref.at[1], in_sem.at[6]),
    ]
    half = rows // 2
    k_copy = pltpu.make_async_copy(k_hbm.at[0], k_ref, k_sem)
    v_copy = pltpu.make_async_copy(v_hbm.at[0], v_ref, v_sem)
    model = wh_ref.shape[0]
    chunk = model // CHUNKS
    w_copy = [
        pltpu.make_async_copy(
            wh_hbm.at[0, pl.ds(c * chunk, chunk), :], wh_ref.at[pl.ds(c * chunk, chunk), :], wh_sem
        )
        for c in range(CHUNKS)
    ]
    small[0].start()
    small[1].start()
    k_copy.start()
    v_copy.start()
    barrier = pltpu.get_barrier_semaphore()
    near = [o for o in OFFSETS + [(0, 0)] if 0 in o]
    for dx, dy in near:
        for other in range(2):
            if (dx, dy, other) == (0, 0, 0):
                continue
            pl.semaphore_signal(
                barrier,
                inc=1,
                device_id={"member": (member + other) % 2, "tensor": peer(dx, dy)},
                device_id_type=pl.DeviceIdType.MESH,
            )
    for c in small[2:] + w_copy:
        c.start()

    small[0].wait()
    small[1].wait()
    k_copy.wait()
    slot = row * span + lax.broadcasted_iota(jnp.int32, (heads, span), 1)
    lane = lax.broadcasted_iota(jnp.int32, (heads, depth), 1)
    weights = []
    for r in range(rows):
        s = lax.dot_general(
            q_ref[r], k_ref[r], (((1,), (1,)), ((), ())), preferred_element_type=f32
        ) * (1.0 / depth**0.5)
        live = slot < len_ref[r]
        s = jnp.where(live, s, f32(-1e30))
        top = jnp.max(s, axis=-1, keepdims=True)
        w = jnp.where(live, jnp.exp(s - top), f32(0.0))
        total = jnp.sum(w, axis=-1, keepdims=True)
        weights.append(w.astype(bf16))
        att_send[pl.ds(rows + r, heads, stride=2 * rows), :] = jnp.where(
            lane < depth // 2, top, total
        )
    v_copy.wait()
    for r in range(rows):
        att_send[pl.ds(r, heads, stride=2 * rows), :] = jnp.dot(
            weights[r], v_ref[r], preferred_element_type=f32
        )

    pl.semaphore_wait(barrier, 2 * len(near) - 1)
    block = 4 * rows
    for dy in (2, 1, 3):
        to = (row + dy) % SIDE
        pltpu.make_async_remote_copy(
            src_ref=att_send.at[pl.ds(pl.multiple_of(to * block, block), block), :],
            dst_ref=att_recv.at[SIDE - dy - 1],
            send_sem=att_ssem,
            recv_sem=att_rsem,
            device_id={"tensor": col * SIDE + to},
            device_id_type=pl.DeviceIdType.MESH,
        ).start()
    small[3].wait()
    small[4].wait()
    small[6].wait()
    gain_mine[0] = gain_ref[:, columns(me)]
    gain_mine[1] = gain_ref[:, columns(peer(2, 2))]
    side_copy = [
        pltpu.make_async_remote_copy(
            src_ref=src,
            dst_ref=dst,
            send_sem=side_ssem.at[i],
            recv_sem=side_rsem.at[i],
            device_id={"member": 1 - member},
            device_id_type=pl.DeviceIdType.MESH,
        )
        for i, (src, dst) in enumerate([(res_ref, res_other), (gain_mine, gain_other)])
    ]
    for c in side_copy:
        c.start()
    inv_ref[...] = 1.0 / (gain_ref[...] * gain_ref[...])
    small[5].wait()
    small[2].wait()
    parts = [att_send[pl.ds(pl.multiple_of(row * block, block), block), :]]
    arrival(att_recv, att_rsem).wait()
    for i in range(SIDE - 1):
        parts.append(att_recv[i])
    attended = []
    for h in range(2):
        base = 2 * h * rows
        stats = [p[base + rows : base + 2 * rows] for p in parts]
        peak = functools.reduce(jnp.maximum, stats)
        num, den = 0.0, 0.0
        for p, st in zip(parts, stats):
            scale = jnp.exp(st - peak)[:, 0:1]
            num = num + scale * p[base : base + rows]
            den = den + scale * st[:, depth // 2 : depth // 2 + 1]
        attended.append(num / den)
    attended = jnp.concatenate(attended, axis=1).astype(bf16)

    def project(t):
        return jnp.dot(
            attended,
            wo_ref[:, pl.ds(pl.multiple_of(t * width, width), width)],
            preferred_element_type=f32,
        )

    def send_pair(dx, dy):
        pltpu.make_async_remote_copy(
            src_ref=rs_send.at[slot_of(dx, dy)],
            dst_ref=rs_recv.at[slot_of(-dx, -dy)],
            send_sem=rs_ssem,
            recv_sem=rs_rsem,
            device_id={"member": 1 - member, "tensor": peer(dx, dy)},
            device_id_type=pl.DeviceIdType.MESH,
        ).start()

    later = []
    for dx, dy in OFFSETS:
        far, near = (dx, dy), ((dx + 2) % SIDE, (dy + 2) % SIDE)
        if near in later or far in later:
            continue
        far_part = project(peer(*far)).astype(bf16)
        near_part = project(peer(*near)).astype(bf16)
        rs_send[slot_of(*far), 0] = far_part
        rs_send[slot_of(*far), 1] = near_part
        rs_send[slot_of(*near), 0] = near_part
        rs_send[slot_of(*near), 1] = far_part
        send_pair(*far)
        later.append(near)
    for near in later:
        send_pair(*near)
    for c in side_copy:
        c.wait_recv()
    hidden = res_other[...].astype(f32)
    arrival(rs_recv, rs_rsem).wait()
    for i in range(rs_recv.shape[0]):
        hidden = hidden + rs_recv[i].astype(f32)
    ag_ref[...] = (hidden * gain_other[...]).astype(bf16)
    mid = REACH[2][0]
    for dx, dy in OFFSETS + [(0, 0)]:
        there, away = slot_of(-dx, -dy), hops(dx, dy)
        if away > 2:
            continue
        pltpu.make_async_remote_copy(
            src_ref=ag_ref.at[0] if away == 2 else ag_ref,
            dst_ref=hg_mid.at[there - mid] if away == 2 else hg_near.at[there],
            send_sem=ag_ssem.at[away // 2],
            recv_sem=ag_rsem.at[away],
            device_id={"member": 1 - member, "tensor": peer(dx, dy)},
            device_id_type=pl.DeviceIdType.MESH,
        ).start()

    arrival(wh_ref, wh_sem).wait()
    logits, square = 0.0, 0.0
    arrived = [hg_near.at[0:1], hg_near.at[1:mid], hg_mid]
    for away in range(3):
        arrival(arrived[away], ag_rsem.at[away]).wait()
        for k in REACH[away]:
            dx, dy = NEAREST[k]
            found = [(peer(dx, dy), hg_mid[k - mid] if away == 2 else hg_near[k, 0])]
            if away < 2:
                found.append((peer(dx + 2, dy + 2), hg_near[k, 1]))
            for t, part in found:
                here = pl.multiple_of(t * width, width)
                logits = logits + jnp.dot(
                    part, wh_ref[pl.ds(here, width), :], preferred_element_type=f32
                )
                wide = part.astype(f32)
                square = square + wide * wide * inv_ref[:, pl.ds(here, width)]
    mean_square = jnp.sum(square, axis=-1, keepdims=True) * (1.0 / model)
    logits = logits * lax.rsqrt(mean_square + 1e-05)
    lg_ref[0] = logits[:half]
    lg_ref[1] = logits[half:]
    lg_copy = pltpu.make_async_remote_copy(
        src_ref=lg_ref.at[1 - member],
        dst_ref=lg_recv,
        send_sem=lg_ssem,
        recv_sem=lg_rsem,
        device_id={"member": 1 - member},
        device_id_type=pl.DeviceIdType.MESH,
    )
    lg_copy.start()

    vocab = logits.shape[1]
    ids = me * vocab + lax.broadcasted_iota(jnp.int32, (rows, vocab), 1)
    sub = lax.broadcasted_iota(jnp.int32, (rows, 1), 0)
    want = jnp.zeros((rows, 1), jnp.int32)
    for r in range(rows):
        want = jnp.where(sub == r, tgt_ref[r], want)
    pick = jnp.sum(jnp.where(ids == want, logits, f32(0.0)), axis=-1, keepdims=True)
    top = jnp.max(logits, axis=-1, keepdims=True)
    lse = top + jnp.log(jnp.sum(jnp.exp(logits - top), axis=-1, keepdims=True))
    lanes = lax.broadcasted_iota(jnp.int32, (rows, 128), 1)
    subs = lax.broadcasted_iota(jnp.int32, (rows, 128), 0)
    spread = jnp.where(lanes < 64, lse, pick)
    stat_ref[0:1] = jnp.sum(
        jnp.where(lanes // 8 % 8 == subs, spread, f32(0.0)), axis=0, keepdims=True
    )
    for dx, dy in OFFSETS + [(0, 0)]:
        for other in range(2):
            there = slot_of(-dx, -dy) + SIDE * SIDE * other
            if there == 0:
                continue
            pltpu.make_async_remote_copy(
                src_ref=stat_ref.at[0:1],
                dst_ref=stat_ref.at[there : there + 1],
                send_sem=st_ssem,
                recv_sem=st_rsem,
                device_id={"member": (member + other) % 2, "tensor": peer(dx, dy)},
                device_id_type=pl.DeviceIdType.MESH,
            ).start()
    lg_copy.wait_recv()
    mean_logits = 0.5 * (lg_ref[member] + lg_recv[...])
    got_stats = stat_ref.at[pl.ds(1, stat_ref.shape[0] - 1)]
    arrival(got_stats, st_rsem).wait()
    log_total, target = 0.0, 0.0
    for other in range(2):
        got = stat_ref[other * SIDE * SIDE : (other + 1) * SIDE * SIDE]
        peak = jnp.max(got, axis=0, keepdims=True)
        total = jnp.sum(jnp.exp(got - peak), axis=0, keepdims=True)
        log_total = log_total + 0.5 * (peak + jnp.log(total))
        target = target + 0.5 * jnp.sum(got, axis=0, keepdims=True)
    lanes = lax.broadcasted_iota(jnp.int32, (half, 128), 1)
    mine = 8 * (member * half + lax.broadcasted_iota(jnp.int32, (half, 128), 0))
    shift = jnp.sum(jnp.where(lanes == mine, log_total, f32(0.0)), axis=-1, keepdims=True)
    chosen = jnp.sum(jnp.where(lanes == mine + 64, target, f32(0.0)), axis=-1, keepdims=True)
    out_ref[...] = mean_logits - shift
    tout_ref[...] = (chosen - shift)[:, 0]

    arrival(att_recv, att_ssem).wait()
    arrival(rs_send, rs_ssem).wait()
    arrival(hg_near, ag_ssem.at[0]).wait()
    arrival(hg_mid, ag_ssem.at[1]).wait()
    arrival(got_stats, st_ssem).wait()
    for c in side_copy + [lg_copy]:
        c.wait_send()


def write_out(out_ref, target_ref, out_hbm, target_hbm, out_sem, target_sem):
    copies = [
        pltpu.make_async_copy(out_ref, out_hbm, out_sem),
        pltpu.make_async_copy(target_ref, target_hbm, target_sem),
    ]
    for c in copies:
        c.start()
    for c in copies:
        c.wait()


def local(queries, keys, values, lengths, targets, residual, out_weight, norm_gain, head_weight):
    rows, span, depth = keys.shape[1:]
    width, model = out_weight.shape[1:]
    vocab = head_weight.shape[2]
    peers = SIDE * SIDE - 1
    heads = HEADS // KV_HEADS
    f32, bf16 = jnp.float32, jnp.bfloat16
    dma = pltpu.SemaphoreType.DMA
    out, target = pl.pallas_call(
        step_kernel,
        out_shape=(
            jax.ShapeDtypeStruct((rows // 2, vocab), f32),
            jax.ShapeDtypeStruct((rows // 2,), f32),
        ),
        in_specs=[pl.BlockSpec(memory_space=HBM)] * 9,
        out_specs=(
            pl.BlockSpec(memory_space=pltpu.MemorySpace.VMEM),
            pl.BlockSpec(memory_space=pltpu.MemorySpace.VMEM),
        ),
        scratch_shapes=[
            pltpu.VMEM((rows, heads, depth), bf16),
            pltpu.VMEM((rows, span, depth), bf16),
            pltpu.VMEM((rows, span, depth), bf16),
            pltpu.SMEM((rows,), jnp.int32),
            pltpu.SMEM((rows,), jnp.int32),
            pltpu.VMEM((2, rows, width), bf16),
            pltpu.VMEM((width, model), bf16),
            pltpu.VMEM((1, model), f32),
            pltpu.VMEM((1, model), f32),
            pltpu.VMEM((model, vocab), bf16),
            pltpu.VMEM((2, rows, width), bf16),
            pltpu.VMEM((2, 1, width), f32),
            pltpu.VMEM((2, 1, width), f32),
            pltpu.VMEM((2 * heads * rows, depth), f32),
            pltpu.VMEM((SIDE - 1, 4 * rows, depth), f32),
            pltpu.VMEM((peers + 1, 2, rows, width), bf16),
            pltpu.VMEM((peers + 1, 2, rows, width), bf16),
            pltpu.VMEM((2, rows, width), bf16),
            pltpu.VMEM((len(REACH[0] + REACH[1]), 2, rows, width), bf16),
            pltpu.VMEM((len(REACH[2]), rows, width), bf16),
            pltpu.VMEM((2, rows // 2, vocab), f32),
            pltpu.VMEM((rows // 2, vocab), f32),
            pltpu.VMEM((2 * (peers + 1), 128), f32),
            dma((7,)), dma, dma, dma,
            dma((2,)), dma((2,)), dma, dma,
            dma, dma,
            dma((2,)), dma((3,)),
            dma, dma,
            dma, dma,
        ],
        compiler_params=pltpu.CompilerParams(
            collective_id=0, has_side_effects=True, vmem_limit_bytes=48 << 20
        ),
        name="decode_step",
    )(*(pltpu.with_memory_space_constraint(a, HBM) for a in (queries, keys, values, lengths, targets, residual, out_weight, norm_gain, head_weight)))
    return pl.pallas_call(
        write_out,
        out_shape=(
            jax.ShapeDtypeStruct((rows // 2, vocab), f32),
            jax.ShapeDtypeStruct((rows // 2,), f32),
        ),
        in_specs=[pl.BlockSpec(memory_space=pltpu.MemorySpace.VMEM)] * 2,
        out_specs=(pl.BlockSpec(memory_space=HBM), pl.BlockSpec(memory_space=HBM)),
        scratch_shapes=[dma, dma],
        compiler_params=pltpu.CompilerParams(vmem_limit_bytes=1 << 20),
        name="write_out",
    )(out, target)


def solution(mesh):
    placed = (
        P("member", "rep", None, None),
        P("member", "rep", "tensor", None),
        P("member", "rep", "tensor", None),
        P("rep"),
        P("rep"),
        P("member", "rep", None),
        P("member", "tensor", None),
        P("member", None),
        P("member", None, "tensor"),
    )
    return jax.shard_map(
        local,
        mesh=mesh,
        in_specs=placed,
        out_specs=(P(("rep", "member"), "tensor"), P(("rep", "member"))),
        check_vma=False,
    )
```

```python
import functools

import jax
import jax.numpy as jnp
from jax import lax
from jax.experimental import pallas as pl
from jax.experimental.pallas import tpu as pltpu
from jax.sharding import PartitionSpec as P

HEADS = 32
KV_HEADS = 4
SIDE = 4
CHUNKS = 4
HBM = pltpu.MemorySpace.HBM


def hops(dx, dy):
    return min(dx, SIDE - dx) + min(dy, SIDE - dy)


OFFSETS = sorted(
    [(dx, dy) for dx in range(SIDE) for dy in range(SIDE) if (dx, dy) != (0, 0)],
    key=lambda o: -hops(*o),
)


NEAREST = [(0, 0)] + OFFSETS[::-1]
SLOT = {o: i for i, o in enumerate(NEAREST)}
REACH = [[i for i, o in enumerate(NEAREST) if hops(*o) == n] for n in range(SIDE + 1)]


HALF_MID = len(REACH[2]) // 2


def slot_of(dx, dy):
    return SLOT[dx % SIDE, dy % SIDE]


def arrival(ref, sem):
    return pltpu.make_async_copy(ref, ref, sem)


def step_kernel(
    q_hbm, k_hbm, v_hbm, len_hbm, tgt_hbm, res_hbm, wo_hbm, gain_hbm, wh_hbm,
    out_ref, tout_ref,
    q_ref, k_ref, v_ref, len_ref, tgt_ref, res_ref, wo_ref, gain_ref, inv_ref, wh_ref,
    res_other, gain_mine, gain_other, att_send, att_recv, rs_send, rs_recv, ag_ref, hg_near, hg_mid, lg_ref, lg_recv, stat_ref,
    in_sem, k_sem, v_sem, wh_sem,
    side_ssem, side_rsem, att_ssem, att_rsem, rs_ssem, rs_rsem, ag_ssem, ag_rsem, lg_ssem, lg_rsem, st_ssem, st_rsem,
):
    me = lax.axis_index("tensor")
    member = lax.axis_index("member")
    col, row = me // SIDE, me % SIDE
    rows, span, depth = k_ref.shape
    heads = HEADS // KV_HEADS
    width = wo_ref.shape[0]
    f32, bf16 = jnp.float32, jnp.bfloat16

    def peer(dx, dy):
        return (col + dx % SIDE) % SIDE * SIDE + (row + dy % SIDE) % SIDE

    def columns(t):
        return pl.ds(pl.multiple_of(t * width, width), width)

    small = [
        pltpu.make_async_copy(q_hbm.at[0, :, pl.ds(col * heads, heads), :], q_ref, in_sem.at[0]),
        pltpu.make_async_copy(len_hbm, len_ref, in_sem.at[1]),
        pltpu.make_async_copy(tgt_hbm, tgt_ref, in_sem.at[2]),
        pltpu.make_async_copy(res_hbm.at[0, :, columns(me)], res_ref.at[0], in_sem.at[3]),
        pltpu.make_async_copy(gain_hbm, gain_ref, in_sem.at[4]),
        pltpu.make_async_copy(wo_hbm.at[0], wo_ref, in_sem.at[5]),
        pltpu.make_async_copy(res_hbm.at[0, :, columns(peer(2, 2))], res_ref.at[1], in_sem.at[6]),
    ]
    half = rows // 2
    k_copy = pltpu.make_async_copy(k_hbm.at[0], k_ref, k_sem)
    v_copy = pltpu.make_async_copy(v_hbm.at[0], v_ref, v_sem)
    model = wh_ref.shape[0]
    chunk = model // CHUNKS
    w_copy = [
        pltpu.make_async_copy(
            wh_hbm.at[0, pl.ds(c * chunk, chunk), :], wh_ref.at[pl.ds(c * chunk, chunk), :], wh_sem
        )
        for c in range(CHUNKS)
    ]
    small[0].start()
    small[1].start()
    k_copy.start()
    v_copy.start()
    barrier = pltpu.get_barrier_semaphore()
    near = [o for o in OFFSETS + [(0, 0)] if 0 in o]
    for dx, dy in near:
        for other in range(2):
            if (dx, dy, other) == (0, 0, 0):
                continue
            pl.semaphore_signal(
                barrier,
                inc=1,
                device_id={"member": (member + other) % 2, "tensor": peer(dx, dy)},
                device_id_type=pl.DeviceIdType.MESH,
            )
    for c in small[2:] + w_copy:
        c.start()

    small[0].wait()
    small[1].wait()
    k_copy.wait()
    slot = row * span + lax.broadcasted_iota(jnp.int32, (heads, span), 1)
    lane = lax.broadcasted_iota(jnp.int32, (heads, depth), 1)
    weights = []
    for r in range(rows):
        s = lax.dot_general(
            q_ref[r], k_ref[r], (((1,), (1,)), ((), ())), preferred_element_type=f32
        ) * (1.0 / depth**0.5)
        live = slot < len_ref[r]
        s = jnp.where(live, s, f32(-1e30))
        top = jnp.max(s, axis=-1, keepdims=True)
        w = jnp.where(live, jnp.exp(s - top), f32(0.0))
        total = jnp.sum(w, axis=-1, keepdims=True)
        weights.append(w.astype(bf16))
        att_send[pl.ds(rows + r, heads, stride=2 * rows), :] = jnp.where(
            lane < depth // 2, top, total
        )
    v_copy.wait()
    for r in range(rows):
        att_send[pl.ds(r, heads, stride=2 * rows), :] = jnp.dot(
            weights[r], v_ref[r], preferred_element_type=f32
        )

    pl.semaphore_wait(barrier, 2 * len(near) - 1)
    block = 4 * rows
    for dy in (2, 1, 3):
        to = (row + dy) % SIDE
        pltpu.make_async_remote_copy(
            src_ref=att_send.at[pl.ds(pl.multiple_of(to * block, block), block), :],
            dst_ref=att_recv.at[SIDE - dy - 1],
            send_sem=att_ssem,
            recv_sem=att_rsem,
            device_id={"tensor": col * SIDE + to},
            device_id_type=pl.DeviceIdType.MESH,
        ).start()
    small[3].wait()
    small[4].wait()
    small[6].wait()
    gain_mine[0] = gain_ref[:, columns(me)]
    gain_mine[1] = gain_ref[:, columns(peer(2, 2))]
    side_copy = [
        pltpu.make_async_remote_copy(
            src_ref=src,
            dst_ref=dst,
            send_sem=side_ssem.at[i],
            recv_sem=side_rsem.at[i],
            device_id={"member": 1 - member},
            device_id_type=pl.DeviceIdType.MESH,
        )
        for i, (src, dst) in enumerate([(res_ref, res_other), (gain_mine, gain_other)])
    ]
    for c in side_copy:
        c.start()
    inv_ref[...] = 1.0 / (gain_ref[...] * gain_ref[...])
    small[5].wait()
    small[2].wait()
    parts = [att_send[pl.ds(pl.multiple_of(row * block, block), block), :]]
    arrival(att_recv, att_rsem).wait()
    for i in range(SIDE - 1):
        parts.append(att_recv[i])
    attended = []
    for h in range(2):
        base = 2 * h * rows
        stats = [p[base + rows : base + 2 * rows] for p in parts]
        peak = functools.reduce(jnp.maximum, stats)
        num, den = 0.0, 0.0
        for p, st in zip(parts, stats):
            scale = jnp.exp(st - peak)[:, 0:1]
            num = num + scale * p[base : base + rows]
            den = den + scale * st[:, depth // 2 : depth // 2 + 1]
        attended.append(num / den)
    attended = jnp.concatenate(attended, axis=1).astype(bf16)

    def project(t):
        return jnp.dot(
            attended,
            wo_ref[:, pl.ds(pl.multiple_of(t * width, width), width)],
            preferred_element_type=f32,
        )

    def send_pair(dx, dy):
        pltpu.make_async_remote_copy(
            src_ref=rs_send.at[slot_of(dx, dy)],
            dst_ref=rs_recv.at[slot_of(-dx, -dy)],
            send_sem=rs_ssem,
            recv_sem=rs_rsem,
            device_id={"member": 1 - member, "tensor": peer(dx, dy)},
            device_id_type=pl.DeviceIdType.MESH,
        ).start()

    later = []
    for dx, dy in OFFSETS:
        far, near = (dx, dy), ((dx + 2) % SIDE, (dy + 2) % SIDE)
        if near in later or far in later:
            continue
        far_part = project(peer(*far)).astype(bf16)
        near_part = project(peer(*near)).astype(bf16)
        rs_send[slot_of(*far), 0] = far_part
        rs_send[slot_of(*far), 1] = near_part
        rs_send[slot_of(*near), 0] = near_part
        rs_send[slot_of(*near), 1] = far_part
        send_pair(*far)
        later.append(near)
    for near in sorted(later, key=lambda o: -hops(*o)):
        send_pair(*near)
    for c in side_copy:
        c.wait_recv()
    hidden = res_other[...].astype(f32)
    arrival(rs_recv, rs_rsem).wait()
    for i in range(rs_recv.shape[0]):
        hidden = hidden + rs_recv[i].astype(f32)
    ag_ref[...] = (hidden * gain_other[...]).astype(bf16)
    mids = [o for o in OFFSETS if hops(*o) == 2]
    for dx, dy in OFFSETS + [(0, 0)]:
        there, away = slot_of(-dx, -dy), hops(dx, dy)
        order = mids.index((dx, dy)) if away == 2 else 0
        if away > 2:
            continue
        pltpu.make_async_remote_copy(
            src_ref=ag_ref.at[0] if away == 2 else ag_ref,
            dst_ref=hg_mid.at[order] if away == 2 else hg_near.at[there],
            send_sem=ag_ssem.at[away // 2],
            recv_sem=ag_rsem.at[away + order // HALF_MID],
            device_id={"member": 1 - member, "tensor": peer(dx, dy)},
            device_id_type=pl.DeviceIdType.MESH,
        ).start()

    arrival(wh_ref, wh_sem).wait()
    logits, square = 0.0, 0.0
    near = len(REACH[0] + REACH[1])
    groups = [(hg_near.at[0:1], range(1)), (hg_near.at[1:near], range(1, near))]
    for i in range(0, len(mids), HALF_MID):
        groups.append((hg_mid.at[i : i + HALF_MID], mids[i : i + HALF_MID]))
    for away, (arrived, sources) in enumerate(groups):
        arrival(arrived, ag_rsem.at[away]).wait()
        for k in sources:
            if away < 2:
                dx, dy = NEAREST[k]
                found = [(peer(dx, dy), hg_near[k, 0]), (peer(dx + 2, dy + 2), hg_near[k, 1])]
            else:
                found = [(peer(-k[0], -k[1]), hg_mid[mids.index(k)])]
            for t, part in found:
                here = pl.multiple_of(t * width, width)
                logits = logits + jnp.dot(
                    part, wh_ref[pl.ds(here, width), :], preferred_element_type=f32
                )
                wide = part.astype(f32)
                square = square + wide * wide * inv_ref[:, pl.ds(here, width)]
    mean_square = jnp.sum(square, axis=-1, keepdims=True) * (1.0 / model)
    logits = logits * lax.rsqrt(mean_square + 1e-05)
    lg_ref[0] = logits[:half]
    lg_ref[1] = logits[half:]
    lg_copy = pltpu.make_async_remote_copy(
        src_ref=lg_ref.at[1 - member],
        dst_ref=lg_recv,
        send_sem=lg_ssem,
        recv_sem=lg_rsem,
        device_id={"member": 1 - member},
        device_id_type=pl.DeviceIdType.MESH,
    )
    lg_copy.start()

    vocab = logits.shape[1]
    ids = me * vocab + lax.broadcasted_iota(jnp.int32, (rows, vocab), 1)
    sub = lax.broadcasted_iota(jnp.int32, (rows, 1), 0)
    want = jnp.zeros((rows, 1), jnp.int32)
    for r in range(rows):
        want = jnp.where(sub == r, tgt_ref[r], want)
    pick = jnp.sum(jnp.where(ids == want, logits, f32(0.0)), axis=-1, keepdims=True)
    top = jnp.max(logits, axis=-1, keepdims=True)
    lse = top + jnp.log(jnp.sum(jnp.exp(logits - top), axis=-1, keepdims=True))
    lanes = lax.broadcasted_iota(jnp.int32, (rows, 128), 1)
    subs = lax.broadcasted_iota(jnp.int32, (rows, 128), 0)
    spread = jnp.where(lanes < 64, lse, pick)
    stat_ref[0:1] = jnp.sum(
        jnp.where(lanes // 8 % 8 == subs, spread, f32(0.0)), axis=0, keepdims=True
    )
    for dx, dy in OFFSETS + [(0, 0)]:
        for other in (1, 0):
            there = slot_of(-dx, -dy) + SIDE * SIDE * other
            if there == 0:
                continue
            pltpu.make_async_remote_copy(
                src_ref=stat_ref.at[0:1],
                dst_ref=stat_ref.at[there : there + 1],
                send_sem=st_ssem,
                recv_sem=st_rsem,
                device_id={"member": (member + other) % 2, "tensor": peer(dx, dy)},
                device_id_type=pl.DeviceIdType.MESH,
            ).start()
    lg_copy.wait_recv()
    mean_logits = 0.5 * (lg_ref[member] + lg_recv[...])
    got_stats = stat_ref.at[pl.ds(1, stat_ref.shape[0] - 1)]
    arrival(got_stats, st_rsem).wait()
    log_total, target = 0.0, 0.0
    for other in range(2):
        got = stat_ref[other * SIDE * SIDE : (other + 1) * SIDE * SIDE]
        peak = jnp.max(got, axis=0, keepdims=True)
        total = jnp.sum(jnp.exp(got - peak), axis=0, keepdims=True)
        log_total = log_total + 0.5 * (peak + jnp.log(total))
        target = target + 0.5 * jnp.sum(got, axis=0, keepdims=True)
    lanes = lax.broadcasted_iota(jnp.int32, (half, 128), 1)
    mine = 8 * (member * half + lax.broadcasted_iota(jnp.int32, (half, 128), 0))
    shift = jnp.sum(jnp.where(lanes == mine, log_total, f32(0.0)), axis=-1, keepdims=True)
    chosen = jnp.sum(jnp.where(lanes == mine + 64, target, f32(0.0)), axis=-1, keepdims=True)
    out_ref[...] = mean_logits - shift
    tout_ref[...] = (chosen - shift)[:, 0]

    arrival(att_recv, att_ssem).wait()
    arrival(rs_send, rs_ssem).wait()
    arrival(hg_near, ag_ssem.at[0]).wait()
    arrival(hg_mid, ag_ssem.at[1]).wait()
    arrival(got_stats, st_ssem).wait()
    for c in side_copy + [lg_copy]:
        c.wait_send()


def write_out(out_ref, target_ref, out_hbm, target_hbm, out_sem, target_sem):
    copies = [
        pltpu.make_async_copy(out_ref, out_hbm, out_sem),
        pltpu.make_async_copy(target_ref, target_hbm, target_sem),
    ]
    for c in copies:
        c.start()
    for c in copies:
        c.wait()


def local(queries, keys, values, lengths, targets, residual, out_weight, norm_gain, head_weight):
    rows, span, depth = keys.shape[1:]
    width, model = out_weight.shape[1:]
    vocab = head_weight.shape[2]
    peers = SIDE * SIDE - 1
    heads = HEADS // KV_HEADS
    f32, bf16 = jnp.float32, jnp.bfloat16
    dma = pltpu.SemaphoreType.DMA
    out, target = pl.pallas_call(
        step_kernel,
        out_shape=(
            jax.ShapeDtypeStruct((rows // 2, vocab), f32),
            jax.ShapeDtypeStruct((rows // 2,), f32),
        ),
        in_specs=[pl.BlockSpec(memory_space=HBM)] * 9,
        out_specs=(
            pl.BlockSpec(memory_space=pltpu.MemorySpace.VMEM),
            pl.BlockSpec(memory_space=pltpu.MemorySpace.VMEM),
        ),
        scratch_shapes=[
            pltpu.VMEM((rows, heads, depth), bf16),
            pltpu.VMEM((rows, span, depth), bf16),
            pltpu.VMEM((rows, span, depth), bf16),
            pltpu.SMEM((rows,), jnp.int32),
            pltpu.SMEM((rows,), jnp.int32),
            pltpu.VMEM((2, rows, width), bf16),
            pltpu.VMEM((width, model), bf16),
            pltpu.VMEM((1, model), f32),
            pltpu.VMEM((1, model), f32),
            pltpu.VMEM((model, vocab), bf16),
            pltpu.VMEM((2, rows, width), bf16),
            pltpu.VMEM((2, 1, width), f32),
            pltpu.VMEM((2, 1, width), f32),
            pltpu.VMEM((2 * heads * rows, depth), f32),
            pltpu.VMEM((SIDE - 1, 4 * rows, depth), f32),
            pltpu.VMEM((peers + 1, 2, rows, width), bf16),
            pltpu.VMEM((peers + 1, 2, rows, width), bf16),
            pltpu.VMEM((2, rows, width), bf16),
            pltpu.VMEM((len(REACH[0] + REACH[1]), 2, rows, width), bf16),
            pltpu.VMEM((len(REACH[2]), rows, width), bf16),
            pltpu.VMEM((2, rows // 2, vocab), f32),
            pltpu.VMEM((rows // 2, vocab), f32),
            pltpu.VMEM((2 * (peers + 1), 128), f32),
            dma((7,)), dma, dma, dma,
            dma((2,)), dma((2,)), dma, dma,
            dma, dma,
            dma((2,)), dma((2 + len(REACH[2]) // HALF_MID,)),
            dma, dma,
            dma, dma,
        ],
        compiler_params=pltpu.CompilerParams(
            collective_id=0, has_side_effects=True, vmem_limit_bytes=48 << 20
        ),
        name="decode_step",
    )(*(pltpu.with_memory_space_constraint(a, HBM) for a in (queries, keys, values, lengths, targets, residual, out_weight, norm_gain, head_weight)))
    return pl.pallas_call(
        write_out,
        out_shape=(
            jax.ShapeDtypeStruct((rows // 2, vocab), f32),
            jax.ShapeDtypeStruct((rows // 2,), f32),
        ),
        in_specs=[pl.BlockSpec(memory_space=pltpu.MemorySpace.VMEM)] * 2,
        out_specs=(pl.BlockSpec(memory_space=HBM), pl.BlockSpec(memory_space=HBM)),
        scratch_shapes=[dma, dma],
        compiler_params=pltpu.CompilerParams(vmem_limit_bytes=1 << 20),
        name="write_out",
    )(out, target)


def solution(mesh):
    placed = (
        P("member", "rep", None, None),
        P("member", "rep", "tensor", None),
        P("member", "rep", "tensor", None),
        P("rep"),
        P("rep"),
        P("member", "rep", None),
        P("member", "tensor", None),
        P("member", None),
        P("member", None, "tensor"),
    )
    return jax.shard_map(
        local,
        mesh=mesh,
        in_specs=placed,
        out_specs=(P(("rep", "member"), "tensor"), P(("rep", "member"))),
        check_vma=False,
    )
```

```python
import functools

import jax
import jax.numpy as jnp
from jax import lax
from jax.experimental import pallas as pl
from jax.experimental.pallas import tpu as pltpu
from jax.sharding import PartitionSpec as P

HEADS = 32
KV_HEADS = 4
SIDE = 4
CHUNKS = 4
HBM = pltpu.MemorySpace.HBM


def hops(dx, dy):
    return min(dx, SIDE - dx) + min(dy, SIDE - dy)


OFFSETS = sorted(
    [(dx, dy) for dx in range(SIDE) for dy in range(SIDE) if (dx, dy) != (0, 0)],
    key=lambda o: -hops(*o),
)


NEAREST = [(0, 0)] + OFFSETS[::-1]
SLOT = {o: i for i, o in enumerate(NEAREST)}
REACH = [[i for i, o in enumerate(NEAREST) if hops(*o) == n] for n in range(SIDE + 1)]


def slot_of(dx, dy):
    return SLOT[dx % SIDE, dy % SIDE]


def arrival(ref, sem):
    return pltpu.make_async_copy(ref, ref, sem)


def step_kernel(
    q_hbm, k_hbm, v_hbm, len_hbm, tgt_hbm, res_hbm, wo_hbm, gain_hbm, wh_hbm,
    out_ref, tout_ref,
    q_ref, k_ref, v_ref, len_ref, tgt_ref, res_ref, wo_ref, gain_ref, inv_ref, wh_ref,
    res_other, gain_mine, gain_other, att_send, att_recv, rs_send, rs_recv, ag_ref, hg_near, hg_mid, lg_ref, lg_recv, stat_ref,
    in_sem, k_sem, v_sem, wh_sem,
    side_ssem, side_rsem, att_ssem, att_rsem, rs_ssem, rs_rsem, ag_ssem, ag_rsem, lg_ssem, lg_rsem, st_ssem, st_rsem,
):
    me = lax.axis_index("tensor")
    member = lax.axis_index("member")
    col, row = me // SIDE, me % SIDE
    rows, span, depth = k_ref.shape
    heads = HEADS // KV_HEADS
    width = wo_ref.shape[0]
    f32, bf16 = jnp.float32, jnp.bfloat16

    def peer(dx, dy):
        return (col + dx) % SIDE * SIDE + (row + dy) % SIDE

    def columns(t):
        return pl.ds(pl.multiple_of(t * width, width), width)

    small = [
        pltpu.make_async_copy(q_hbm.at[0, :, pl.ds(col * heads, heads), :], q_ref, in_sem.at[0]),
        pltpu.make_async_copy(len_hbm, len_ref, in_sem.at[1]),
        pltpu.make_async_copy(tgt_hbm, tgt_ref, in_sem.at[2]),
        pltpu.make_async_copy(res_hbm.at[0, :, columns(me)], res_ref.at[0], in_sem.at[3]),
        pltpu.make_async_copy(gain_hbm, gain_ref, in_sem.at[4]),
        pltpu.make_async_copy(wo_hbm.at[0], wo_ref, in_sem.at[5]),
        pltpu.make_async_copy(res_hbm.at[0, :, columns(peer(2, 2))], res_ref.at[1], in_sem.at[6]),
    ]
    half = rows // 2
    k_copy = pltpu.make_async_copy(k_hbm.at[0], k_ref, k_sem)
    v_copy = pltpu.make_async_copy(v_hbm.at[0], v_ref, v_sem)
    model = wh_ref.shape[0]
    chunk = model // CHUNKS
    w_copy = [
        pltpu.make_async_copy(
            wh_hbm.at[0, pl.ds(c * chunk, chunk), :], wh_ref.at[pl.ds(c * chunk, chunk), :], wh_sem
        )
        for c in range(CHUNKS)
    ]
    small[0].start()
    small[1].start()
    k_copy.start()
    v_copy.start()
    for c in small[2:] + w_copy:
        c.start()

    barrier = pltpu.get_barrier_semaphore()
    near = [o for o in OFFSETS + [(0, 0)] if 0 in o]
    for dx, dy in near:
        for other in range(2):
            if (dx, dy, other) == (0, 0, 0):
                continue
            pl.semaphore_signal(
                barrier,
                inc=1,
                device_id={"member": (member + other) % 2, "tensor": peer(dx, dy)},
                device_id_type=pl.DeviceIdType.MESH,
            )

    small[0].wait()
    small[1].wait()
    k_copy.wait()
    slot = row * span + lax.broadcasted_iota(jnp.int32, (heads, span), 1)
    lane = lax.broadcasted_iota(jnp.int32, (heads, depth), 1)
    weights = []
    for r in range(rows):
        s = lax.dot_general(
            q_ref[r], k_ref[r], (((1,), (1,)), ((), ())), preferred_element_type=f32
        ) * (1.0 / depth**0.5)
        live = slot < len_ref[r]
        s = jnp.where(live, s, f32(-1e30))
        top = jnp.max(s, axis=-1, keepdims=True)
        w = jnp.where(live, jnp.exp(s - top), f32(0.0))
        total = jnp.sum(w, axis=-1, keepdims=True)
        weights.append(w.astype(bf16))
        att_send[pl.ds(rows + r, heads, stride=2 * rows), :] = jnp.where(
            lane < depth // 2, top, total
        )
    v_copy.wait()
    for r in range(rows):
        att_send[pl.ds(r, heads, stride=2 * rows), :] = jnp.dot(
            weights[r], v_ref[r], preferred_element_type=f32
        )

    pl.semaphore_wait(barrier, 2 * len(near) - 1)
    block = 4 * rows
    for dy in (2, 1, 3):
        to = (row + dy) % SIDE
        pltpu.make_async_remote_copy(
            src_ref=att_send.at[pl.ds(pl.multiple_of(to * block, block), block), :],
            dst_ref=att_recv.at[SIDE - dy - 1],
            send_sem=att_ssem,
            recv_sem=att_rsem,
            device_id={"tensor": col * SIDE + to},
            device_id_type=pl.DeviceIdType.MESH,
        ).start()
    small[3].wait()
    small[4].wait()
    small[6].wait()
    gain_mine[0] = gain_ref[:, columns(me)]
    gain_mine[1] = gain_ref[:, columns(peer(2, 2))]
    side_copy = [
        pltpu.make_async_remote_copy(
            src_ref=src,
            dst_ref=dst,
            send_sem=side_ssem.at[i],
            recv_sem=side_rsem.at[i],
            device_id={"member": 1 - member},
            device_id_type=pl.DeviceIdType.MESH,
        )
        for i, (src, dst) in enumerate([(res_ref, res_other), (gain_mine, gain_other)])
    ]
    for c in side_copy:
        c.start()
    inv_ref[...] = 1.0 / (gain_ref[...] * gain_ref[...])
    small[5].wait()
    small[2].wait()
    parts = [att_send[pl.ds(pl.multiple_of(row * block, block), block), :]]
    arrival(att_recv, att_rsem).wait()
    for i in range(SIDE - 1):
        parts.append(att_recv[i])
    attended = []
    for h in range(2):
        base = 2 * h * rows
        stats = [p[base + rows : base + 2 * rows] for p in parts]
        peak = functools.reduce(jnp.maximum, stats)
        num, den = 0.0, 0.0
        for p, st in zip(parts, stats):
            scale = jnp.exp(st - peak)[:, 0:1]
            num = num + scale * p[base : base + rows]
            den = den + scale * st[:, depth // 2 : depth // 2 + 1]
        attended.append(num / den)
    attended = jnp.concatenate(attended, axis=1).astype(bf16)

    def project(t):
        return jnp.dot(
            attended,
            wo_ref[:, pl.ds(pl.multiple_of(t * width, width), width)],
            preferred_element_type=f32,
        )

    def send_pair(dx, dy):
        pltpu.make_async_remote_copy(
            src_ref=rs_send.at[slot_of(dx, dy)],
            dst_ref=rs_recv.at[slot_of(-dx, -dy)],
            send_sem=rs_ssem,
            recv_sem=rs_rsem,
            device_id={"member": 1 - member, "tensor": peer(dx, dy)},
            device_id_type=pl.DeviceIdType.MESH,
        ).start()

    later = []
    for dx, dy in OFFSETS:
        far, near = (dx, dy), ((dx + 2) % SIDE, (dy + 2) % SIDE)
        if near in later or far in later:
            continue
        far_part = project(peer(*far)).astype(bf16)
        near_part = project(peer(*near)).astype(bf16)
        rs_send[slot_of(*far), 0] = far_part
        rs_send[slot_of(*far), 1] = near_part
        rs_send[slot_of(*near), 0] = near_part
        rs_send[slot_of(*near), 1] = far_part
        send_pair(*far)
        later.append(near)
    for near in later:
        send_pair(*near)
    for c in side_copy:
        c.wait_recv()
    hidden = res_other[...].astype(f32)
    arrival(rs_recv, rs_rsem).wait()
    for i in range(rs_recv.shape[0]):
        hidden = hidden + rs_recv[i].astype(f32)
    ag_ref[...] = (hidden * gain_other[...]).astype(bf16)
    mid = REACH[2][0]
    for dx, dy in OFFSETS + [(0, 0)]:
        there, away = slot_of(-dx, -dy), hops(dx, dy)
        if away > 2:
            continue
        pltpu.make_async_remote_copy(
            src_ref=ag_ref.at[0] if away == 2 else ag_ref,
            dst_ref=hg_mid.at[there - mid] if away == 2 else hg_near.at[there],
            send_sem=ag_ssem.at[away // 2],
            recv_sem=ag_rsem.at[away],
            device_id={"member": 1 - member, "tensor": peer(dx, dy)},
            device_id_type=pl.DeviceIdType.MESH,
        ).start()

    arrival(wh_ref, wh_sem).wait()
    logits, square = 0.0, 0.0
    arrived = [hg_near.at[0:1], hg_near.at[1:mid], hg_mid]
    for away in range(3):
        arrival(arrived[away], ag_rsem.at[away]).wait()
        for k in REACH[away]:
            dx, dy = NEAREST[k]
            found = [(peer(dx, dy), hg_mid[k - mid] if away == 2 else hg_near[k, 0])]
            if away < 2:
                found.append((peer(dx + 2, dy + 2), hg_near[k, 1]))
            for t, part in found:
                here = pl.multiple_of(t * width, width)
                logits = logits + jnp.dot(
                    part, wh_ref[pl.ds(here, width), :], preferred_element_type=f32
                )
                wide = part.astype(f32)
                square = square + wide * wide * inv_ref[:, pl.ds(here, width)]
    mean_square = jnp.sum(square, axis=-1, keepdims=True) * (1.0 / model)
    logits = logits * lax.rsqrt(mean_square + 1e-05)
    lg_ref[0] = logits[:half]
    lg_ref[1] = logits[half:]
    lg_copy = pltpu.make_async_remote_copy(
        src_ref=lg_ref.at[1 - member],
        dst_ref=lg_recv,
        send_sem=lg_ssem,
        recv_sem=lg_rsem,
        device_id={"member": 1 - member},
        device_id_type=pl.DeviceIdType.MESH,
    )
    lg_copy.start()

    vocab = logits.shape[1]
    ids = me * vocab + lax.broadcasted_iota(jnp.int32, (rows, vocab), 1)
    sub = lax.broadcasted_iota(jnp.int32, (rows, 1), 0)
    want = jnp.zeros((rows, 1), jnp.int32)
    for r in range(rows):
        want = jnp.where(sub == r, tgt_ref[r], want)
    pick = jnp.sum(jnp.where(ids == want, logits, f32(0.0)), axis=-1, keepdims=True)
    top = jnp.max(logits, axis=-1, keepdims=True)
    lse = top + jnp.log(jnp.sum(jnp.exp(logits - top), axis=-1, keepdims=True))
    lanes = lax.broadcasted_iota(jnp.int32, (rows, 128), 1)
    subs = lax.broadcasted_iota(jnp.int32, (rows, 128), 0)
    spread = jnp.where(lanes < 64, lse, pick)
    stat_ref[0:1] = jnp.sum(
        jnp.where(lanes // 8 % 8 == subs, spread, f32(0.0)), axis=0, keepdims=True
    )
    for dx, dy in OFFSETS + [(0, 0)]:
        for other in range(2):
            there = slot_of(-dx, -dy) + SIDE * SIDE * other
            if there == 0:
                continue
            pltpu.make_async_remote_copy(
                src_ref=stat_ref.at[0:1],
                dst_ref=stat_ref.at[there : there + 1],
                send_sem=st_ssem,
                recv_sem=st_rsem,
                device_id={"member": (member + other) % 2, "tensor": peer(dx, dy)},
                device_id_type=pl.DeviceIdType.MESH,
            ).start()
    lg_copy.wait_recv()
    mean_logits = 0.5 * (lg_ref[member] + lg_recv[...])
    got_stats = stat_ref.at[pl.ds(1, stat_ref.shape[0] - 1)]
    arrival(got_stats, st_rsem).wait()
    log_total, target = 0.0, 0.0
    for other in range(2):
        got = stat_ref[other * SIDE * SIDE : (other + 1) * SIDE * SIDE]
        peak = jnp.max(got, axis=0, keepdims=True)
        total = jnp.sum(jnp.exp(got - peak), axis=0, keepdims=True)
        log_total = log_total + 0.5 * (peak + jnp.log(total))
        target = target + 0.5 * jnp.sum(got, axis=0, keepdims=True)
    lanes = lax.broadcasted_iota(jnp.int32, (half, 128), 1)
    mine = 8 * (member * half + lax.broadcasted_iota(jnp.int32, (half, 128), 0))
    shift = jnp.sum(jnp.where(lanes == mine, log_total, f32(0.0)), axis=-1, keepdims=True)
    chosen = jnp.sum(jnp.where(lanes == mine + 64, target, f32(0.0)), axis=-1, keepdims=True)
    out_ref[...] = mean_logits - shift
    tout_ref[...] = (chosen - shift)[:, 0]

    arrival(att_recv, att_ssem).wait()
    arrival(rs_send, rs_ssem).wait()
    arrival(hg_near, ag_ssem.at[0]).wait()
    arrival(hg_mid, ag_ssem.at[1]).wait()
    arrival(got_stats, st_ssem).wait()
    for c in side_copy + [lg_copy]:
        c.wait_send()


def write_out(out_ref, target_ref, out_hbm, target_hbm, out_sem, target_sem):
    copies = [
        pltpu.make_async_copy(out_ref, out_hbm, out_sem),
        pltpu.make_async_copy(target_ref, target_hbm, target_sem),
    ]
    for c in copies:
        c.start()
    for c in copies:
        c.wait()


def local(queries, keys, values, lengths, targets, residual, out_weight, norm_gain, head_weight):
    rows, span, depth = keys.shape[1:]
    width, model = out_weight.shape[1:]
    vocab = head_weight.shape[2]
    peers = SIDE * SIDE - 1
    heads = HEADS // KV_HEADS
    f32, bf16 = jnp.float32, jnp.bfloat16
    dma = pltpu.SemaphoreType.DMA
    out, target = pl.pallas_call(
        step_kernel,
        out_shape=(
            jax.ShapeDtypeStruct((rows // 2, vocab), f32),
            jax.ShapeDtypeStruct((rows // 2,), f32),
        ),
        in_specs=[pl.BlockSpec(memory_space=HBM)] * 9,
        out_specs=(
            pl.BlockSpec(memory_space=pltpu.MemorySpace.VMEM),
            pl.BlockSpec(memory_space=pltpu.MemorySpace.VMEM),
        ),
        scratch_shapes=[
            pltpu.VMEM((rows, heads, depth), bf16),
            pltpu.VMEM((rows, span, depth), bf16),
            pltpu.VMEM((rows, span, depth), bf16),
            pltpu.SMEM((rows,), jnp.int32),
            pltpu.SMEM((rows,), jnp.int32),
            pltpu.VMEM((2, rows, width), bf16),
            pltpu.VMEM((width, model), bf16),
            pltpu.VMEM((1, model), f32),
            pltpu.VMEM((1, model), f32),
            pltpu.VMEM((model, vocab), bf16),
            pltpu.VMEM((2, rows, width), bf16),
            pltpu.VMEM((2, 1, width), f32),
            pltpu.VMEM((2, 1, width), f32),
            pltpu.VMEM((2 * heads * rows, depth), f32),
            pltpu.VMEM((SIDE - 1, 4 * rows, depth), f32),
            pltpu.VMEM((peers + 1, 2, rows, width), bf16),
            pltpu.VMEM((peers + 1, 2, rows, width), bf16),
            pltpu.VMEM((2, rows, width), bf16),
            pltpu.VMEM((len(REACH[0] + REACH[1]), 2, rows, width), bf16),
            pltpu.VMEM((len(REACH[2]), rows, width), bf16),
            pltpu.VMEM((2, rows // 2, vocab), f32),
            pltpu.VMEM((rows // 2, vocab), f32),
            pltpu.VMEM((2 * (peers + 1), 128), f32),
            dma((7,)), dma, dma, dma,
            dma((2,)), dma((2,)), dma, dma,
            dma, dma,
            dma((2,)), dma((3,)),
            dma, dma,
            dma, dma,
        ],
        compiler_params=pltpu.CompilerParams(
            collective_id=0, has_side_effects=True, vmem_limit_bytes=48 << 20
        ),
        name="decode_step",
    )(*(pltpu.with_memory_space_constraint(a, HBM) for a in (queries, keys, values, lengths, targets, residual, out_weight, norm_gain, head_weight)))
    return pl.pallas_call(
        write_out,
        out_shape=(
            jax.ShapeDtypeStruct((rows // 2, vocab), f32),
            jax.ShapeDtypeStruct((rows // 2,), f32),
        ),
        in_specs=[pl.BlockSpec(memory_space=pltpu.MemorySpace.VMEM)] * 2,
        out_specs=(pl.BlockSpec(memory_space=HBM), pl.BlockSpec(memory_space=HBM)),
        scratch_shapes=[dma, dma],
        compiler_params=pltpu.CompilerParams(vmem_limit_bytes=1 << 20),
        name="write_out",
    )(out, target)


def solution(mesh):
    placed = (
        P("member", "rep", None, None),
        P("member", "rep", "tensor", None),
        P("member", "rep", "tensor", None),
        P("rep"),
        P("rep"),
        P("member", "rep", None),
        P("member", "tensor", None),
        P("member", None),
        P("member", None, "tensor"),
    )
    return jax.shard_map(
        local,
        mesh=mesh,
        in_specs=placed,
        out_specs=(P(("rep", "member"), "tensor"), P(("rep", "member"))),
        check_vma=False,
    )
```
